512 devices in a mesh: dp: 16 (over z, core), mp: 32 (over y, x).
Axes of the slice: x: 4, y: 8, z: 8, core: 2. Of those that a mesh axis runs over, the one named last changes fastest.
Arguments:
- inputs: bfloat16 [32768, 4096], P('dp', 'mp'), may hold values from -6 to 6
- out_grad: bfloat16 [32768, 4096], P('dp', 'mp'), may hold values from -6 to 6
- mean_state: float32 [6, 64, 64, 64], P(None, 'mp', 'dp'), may hold values from -0.75 to 0.75
- hess_state: float32 [6, 64, 64, 64], P(None, 'mp', 'dp'), may hold values from 2 to 20
- grad_state: float32 [6, 64, 64, 64], P(None, 'mp', 'dp'), may hold values from -1.8 to 1.8
- noise_draw: float32 [16, 6, 64, 64, 64], P('dp', None, 'mp'), may hold values from -6 to 6
Outputs:
- new_mean: float32 [6, 64, 64, 64], P(None, 'mp', 'dp')
- new_hess: float32 [6, 64, 64, 64], P(None, 'mp', 'dp')
- new_grad: float32 [6, 64, 64, 64], P(None, 'mp', 'dp')
The draws below stay inside these ranges and needn't reach their ends.
All inputs are finite; a program needn't handle non-finite values.
Results may differ from the reference program's by a relative error of at most 0.0018.
Values may be sent and summed in bfloat16 or wider, within the bound.
No kernel may reach another device: no remote copies, remote signals or barrier semaphores. Data moves between devices by JAX's collectives and lax.ppermute only.
A program may use at most 64 MiB of HBM per device.

```python
import math
import jax
import jax.numpy as jnp
from jax import lax

NB = 64
BS = 64
D = 4096
TOK_DEV = 2048
TOKENS = 32768
N_DP = 16


def block_levels(key, shape, shards, smallest, largest):
    level = 1.0
    for axis_at, parts in shards:
        steps = jax.random.uniform(jax.random.fold_in(jax.random.fold_in(key, 6), axis_at), (parts,), jnp.float32, smallest / len(shards), largest / len(shards))
        level = level * jnp.repeat(jnp.exp(steps), shape[axis_at] // parts).reshape((-1,) + (1,) * (len(shape) - 1 - axis_at))
    return level


def scatter_about(rng, shape, deviation, bound, shards=(), held_as=jnp.bfloat16):
    loudness = block_levels(rng, shape, shards, -0.22, 0.18) if shards else 1.0
    result = jax.random.normal(rng, shape, jnp.float32) * deviation * loudness
    return jnp.minimum(jnp.maximum(result, -bound), bound).astype(held_as)


def setup_inputs(seed: int = 0) -> dict:
    seeds = jax.random.split(jax.random.key(seed), 7)
    return {
        "inputs": scatter_about(seeds[0], (TOKENS, D), 1.0, 6.0, ((0, 16), (1, 32))),
        "out_grad": scatter_about(seeds[1], (TOKENS, D), 1.0, 6.0, ((0, 16), (1, 32))),
        "mean_state": scatter_about(seeds[2], (6, NB, BS, BS), BS ** -0.5, 0.75, ((1, 32), (2, 16)), jnp.float32),
        "hess_state": jnp.clip(jnp.exp(math.log(20.0) - 2.3025851 * jax.random.uniform(seeds[3], (6, NB, BS, BS), jnp.float32) ** block_levels(seeds[3], (6, NB, BS, BS), ((1, 32), (2, 16)), -0.2, 0.2)), 2.0, 20.0),
        "grad_state": scatter_about(seeds[4], (6, NB, BS, BS), 0.3, 1.8, ((1, 32), (2, 16)), jnp.float32),
        "noise_draw": scatter_about(seeds[5], (N_DP, 6, NB, BS, BS), 1.0, 6.0, ((0, 16), (2, 32)), jnp.float32),
    }


LAMBDA_SIZE = 100.0
DELTA_DAMP = 0.001
BETA_GRAD = 0.9
BETA_HESS = 0.9
STEP_RATE = 1.0

def fdot(form, left, right):
    return jnp.einsum(form, left.astype(jnp.float32), right.astype(jnp.float32))

def silu_slope(value):
    sigm = jax.nn.sigmoid(value)
    return sigm * (1.0 + value * (1.0 - sigm))

def reference(inputs, out_grad, mean_state, hess_state, grad_state, noise_draw):
    spread = jnp.sqrt(LAMBDA_SIZE * (hess_state + DELTA_DAMP))
    scale = TOK_DEV ** (-0.5)
    rows_all = inputs.reshape(N_DP, TOK_DEV, NB, BS)
    cots_all = out_grad.reshape(N_DP, TOK_DEV, NB, BS)

    def one_group(item):
        rows, cots, noise = item
        sampled = (mean_state + noise / spread).astype(jnp.bfloat16)
        y_left = fdot('tbr,brc->tbc', rows, sampled[0]).astype(jnp.bfloat16)
        y_right = fdot('tbr,brc->tbc', rows, sampled[2]).astype(jnp.bfloat16)
        perm_left = jnp.transpose(y_left, (0, 2, 1))
        perm_right = jnp.transpose(y_right, (0, 2, 1))
        u_left = fdot('tji,jic->tjc', perm_left, sampled[1])
        u_right = fdot('tji,jic->tjc', perm_right, sampled[3])
        hidden = (jax.nn.silu(u_left) * u_right).astype(jnp.bfloat16)
        outer = fdot('tbr,brc->tbc', hidden, sampled[4]).astype(jnp.bfloat16)
        mixed = jnp.transpose(outer, (0, 2, 1))
        grad_five = fdot('tji,tjc->jic', mixed, cots) * scale
        back_outer = fdot('tjc,jic->tji', cots, sampled[5]).astype(jnp.bfloat16)
        back_hidden = jnp.transpose(back_outer, (0, 2, 1))
        grad_four = fdot('tbr,tbc->brc', hidden, back_hidden) * scale
        d_hidden = fdot('tbc,brc->tbr', back_hidden, sampled[4])
        gate_grad = (d_hidden * u_right * silu_slope(u_left)).astype(jnp.bfloat16)
        value_grad = (d_hidden * jax.nn.silu(u_left)).astype(jnp.bfloat16)
        grad_one = fdot('tji,tjc->jic', perm_left, gate_grad) * scale
        grad_three = fdot('tji,tjc->jic', perm_right, value_grad) * scale
        back_left = fdot('tjc,jic->tji', gate_grad, sampled[1]).astype(jnp.bfloat16)
        back_right = fdot('tjc,jic->tji', value_grad, sampled[3]).astype(jnp.bfloat16)
        rows_left = jnp.transpose(back_left, (0, 2, 1))
        rows_right = jnp.transpose(back_right, (0, 2, 1))
        grad_zero = fdot('tbr,tbc->brc', rows, rows_left) * scale
        grad_two = fdot('tbr,tbc->brc', rows, rows_right) * scale
        grads = jnp.stack([grad_zero, grad_one, grad_two, grad_three, grad_four, grad_five])
        return (grads, grads * noise * spread)
    grads_all, curv_all = lax.map(one_group, (rows_all, cots_all, noise_draw))
    grad_avg = lax.optimization_barrier(jnp.sum(grads_all, axis=0)) / N_DP
    hess_avg = lax.optimization_barrier(jnp.sum(curv_all, axis=0)) / N_DP
    new_grad = BETA_GRAD * grad_state + (1.0 - BETA_GRAD) * grad_avg
    new_hess = BETA_HESS * hess_state + (1.0 - BETA_HESS) * hess_avg + 0.5 * (1.0 - BETA_HESS) ** 2 * (hess_state - hess_avg) ** 2 / (hess_state + DELTA_DAMP)
    new_mean = mean_state - STEP_RATE * (new_grad + DELTA_DAMP * mean_state) / (new_hess + DELTA_DAMP)
    return (new_mean, new_hess, new_grad)
```

```python
import jax
import jax.numpy as jnp
from jax import lax
from jax.sharding import PartitionSpec as P

LAMBDA_SIZE = 100.0
DELTA_DAMP = 0.001
BETA_GRAD = 0.9
BETA_HESS = 0.9
STEP_RATE = 1.0

REDUCE_MODE = "a2a"


def bdot(form, left, right):
    return jnp.einsum(form, left, right, preferred_element_type=jnp.float32)


def silu_slope(value):
    sigm = jax.nn.sigmoid(value)
    return sigm * (1.0 + value * (1.0 - sigm))


def gather_rows(stacked, groups):
    moved = jnp.moveaxis(stacked, 3, 0)
    full = lax.all_gather(moved, "dp", axis=0, tiled=True)
    return jnp.moveaxis(full, 0, 3)


def scatter_rows(stacked, groups):
    s, f, b, r, w = stacked.shape
    split = stacked.reshape(s, f, b, groups, r // groups, w)
    split = jnp.moveaxis(split, 3, 0)
    if REDUCE_MODE == "a2a":
        got = lax.all_to_all(split, "dp", split_axis=0, concat_axis=0, tiled=True)
        summed = jnp.sum(got, axis=0)
    else:
        summed = lax.psum_scatter(split, "dp", scatter_dimension=0, tiled=False)
    return summed


def per_device(inputs, out_grad, mean_state, hess_state, grad_state, noise_draw):
    tokens = inputs.shape[0]
    local_blocks = mean_state.shape[1]
    width = mean_state.shape[3]
    groups = lax.axis_size("dp")
    scale = tokens ** (-0.5)
    full = gather_rows(jnp.stack([mean_state, hess_state]), groups)
    full_mean, full_hess = full[0], full[1]
    spread = jnp.sqrt(LAMBDA_SIZE * (full_hess + DELTA_DAMP))
    noise = noise_draw[0]
    sampled = (full_mean + noise / spread).astype(jnp.bfloat16)
    in_rows = inputs.reshape(tokens, local_blocks, width)
    grad_rows = out_grad.reshape(tokens, local_blocks, width)
    y_left = bdot("tbr,brc->tcb", in_rows, sampled[0]).astype(jnp.bfloat16)
    y_right = bdot("tbr,brc->tcb", in_rows, sampled[2]).astype(jnp.bfloat16)
    back_outer = bdot("tjc,jic->tij", grad_rows, sampled[5]).astype(jnp.bfloat16)
    first = lax.all_to_all(
        jnp.stack([y_left, y_right, back_outer], axis=1), "mp", split_axis=2, concat_axis=3, tiled=True
    )
    perm_left, perm_right, back_hidden = first[:, 0], first[:, 1], first[:, 2]
    u_left = bdot("tji,jic->tjc", perm_left, sampled[1])
    u_right = bdot("tji,jic->tjc", perm_right, sampled[3])
    hidden = (jax.nn.silu(u_left) * u_right).astype(jnp.bfloat16)
    outer = bdot("tbr,brc->tcb", hidden, sampled[4]).astype(jnp.bfloat16)
    grad_four = bdot("tbr,tbc->brc", hidden, back_hidden) * scale
    d_hidden = bdot("tbc,brc->tbr", back_hidden, sampled[4])
    gate_grad = (d_hidden * u_right * silu_slope(u_left)).astype(jnp.bfloat16)
    value_grad = (d_hidden * jax.nn.silu(u_left)).astype(jnp.bfloat16)
    grad_one = bdot("tji,tjc->jic", perm_left, gate_grad) * scale
    grad_three = bdot("tji,tjc->jic", perm_right, value_grad) * scale
    back_left = bdot("tjc,jic->tij", gate_grad, sampled[1]).astype(jnp.bfloat16)
    back_right = bdot("tjc,jic->tij", value_grad, sampled[3]).astype(jnp.bfloat16)
    second = lax.all_to_all(
        jnp.stack([outer, back_left, back_right], axis=1), "mp", split_axis=2, concat_axis=3, tiled=True
    )
    mixed_rows, rows_left, rows_right = second[:, 0], second[:, 1], second[:, 2]
    grad_five = bdot("tji,tjc->jic", mixed_rows, grad_rows) * scale
    grad_zero = bdot("tbr,tbc->brc", in_rows, rows_left) * scale
    grad_two = bdot("tbr,tbc->brc", in_rows, rows_right) * scale
    all_grads = jnp.stack([grad_zero, grad_one, grad_two, grad_three, grad_four, grad_five])
    sums = scatter_rows(jnp.stack([all_grads, all_grads * noise * spread]), groups)
    grad_avg = sums[0] / groups
    hess_avg = sums[1] / groups
    new_grad = BETA_GRAD * grad_state + (1.0 - BETA_GRAD) * grad_avg
    new_hess = (
        BETA_HESS * hess_state
        + (1.0 - BETA_HESS) * hess_avg
        + 0.5 * (1.0 - BETA_HESS) ** 2 * (hess_state - hess_avg) ** 2 / (hess_state + DELTA_DAMP)
    )
    new_mean = mean_state - STEP_RATE * (new_grad + DELTA_DAMP * mean_state) / (
        new_hess + DELTA_DAMP
    )
    return (new_mean, new_hess, new_grad)


def solution(mesh):
    return jax.shard_map(
        per_device,
        mesh=mesh,
        in_specs=(
            P("dp", "mp"),
            P("dp", "mp"),
            P(None, "mp", "dp", None),
            P(None, "mp", "dp", None),
            P(None, "mp", "dp", None),
            P("dp", None, "mp", None, None),
        ),
        out_specs=(P(None, "mp", "dp", None), P(None, "mp", "dp", None), P(None, "mp", "dp", None)),
        check_vma=False,
    )
```

```python
import jax
import jax.numpy as jnp
from jax import lax
from jax.sharding import Mesh, PartitionSpec as P

LAMBDA_SIZE = 100.0
DELTA_DAMP = 0.001
BETA_GRAD = 0.9
BETA_HESS = 0.9
STEP_RATE = 1.0

REDUCE_MODE = "a2a"


def bdot(form, left, right):
    return jnp.einsum(form, left, right, preferred_element_type=jnp.float32)


def silu_slope(value):
    sigm = jax.nn.sigmoid(value)
    return sigm * (1.0 + value * (1.0 - sigm))


def gather_rows(stacked, groups):
    moved = jnp.moveaxis(stacked, 3, 0)
    full = lax.all_gather(moved, "dp", axis=0, tiled=True)
    return jnp.moveaxis(full, 0, 3)


def scatter_rows(stacked, groups):
    s, f, b, r, w = stacked.shape
    split = stacked.reshape(s, f, b, groups, r // groups, w)
    split = jnp.moveaxis(split, 3, 0)
    if REDUCE_MODE == "a2a":
        got = lax.all_to_all(split, "dp", split_axis=0, concat_axis=0, tiled=True)
        summed = jnp.sum(got, axis=0)
    else:
        summed = lax.psum_scatter(split, "dp", scatter_dimension=0, tiled=False)
    return summed


def mp_exchange(send):
    t, s, nb, b = send.shape
    ny, nx = lax.axis_size("my"), lax.axis_size("mx")
    parts = send.reshape(t, s, ny, nx, nb // (ny * nx), b)
    parts = lax.all_to_all(parts, "mx", split_axis=3, concat_axis=3, tiled=False)
    parts = lax.all_to_all(parts, "my", split_axis=2, concat_axis=2, tiled=False)
    parts = jnp.transpose(parts, (0, 1, 4, 2, 3, 5))
    return parts.reshape(t, s, nb // (ny * nx), ny * nx * b)


def per_device(inputs, out_grad, mean_state, hess_state, grad_state, noise_draw):
    tokens = inputs.shape[0]
    local_blocks = mean_state.shape[1]
    width = mean_state.shape[3]
    groups = lax.axis_size("dp")
    scale = tokens ** (-0.5)
    full = gather_rows(jnp.stack([mean_state, hess_state]), groups)
    full_mean, full_hess = full[0], full[1]
    spread = jnp.sqrt(LAMBDA_SIZE * (full_hess + DELTA_DAMP))
    noise = noise_draw[0]
    sampled = (full_mean + noise / spread).astype(jnp.bfloat16)
    in_rows = inputs.reshape(tokens, local_blocks, width)
    grad_rows = out_grad.reshape(tokens, local_blocks, width)
    y_left = bdot("tbr,brc->tcb", in_rows, sampled[0]).astype(jnp.bfloat16)
    y_right = bdot("tbr,brc->tcb", in_rows, sampled[2]).astype(jnp.bfloat16)
    back_outer = bdot("tjc,jic->tij", grad_rows, sampled[5]).astype(jnp.bfloat16)
    first = mp_exchange(jnp.stack([y_left, y_right, back_outer], axis=1))
    perm_left, perm_right, back_hidden = first[:, 0], first[:, 1], first[:, 2]
    u_left = bdot("tji,jic->tjc", perm_left, sampled[1])
    u_right = bdot("tji,jic->tjc", perm_right, sampled[3])
    hidden = (jax.nn.silu(u_left) * u_right).astype(jnp.bfloat16)
    outer = bdot("tbr,brc->tcb", hidden, sampled[4]).astype(jnp.bfloat16)
    grad_four = bdot("tbr,tbc->brc", hidden, back_hidden) * scale
    d_hidden = bdot("tbc,brc->tbr", back_hidden, sampled[4])
    gate_grad = (d_hidden * u_right * silu_slope(u_left)).astype(jnp.bfloat16)
    value_grad = (d_hidden * jax.nn.silu(u_left)).astype(jnp.bfloat16)
    grad_one = bdot("tji,tjc->jic", perm_left, gate_grad) * scale
    grad_three = bdot("tji,tjc->jic", perm_right, value_grad) * scale
    back_left = bdot("tjc,jic->tij", gate_grad, sampled[1]).astype(jnp.bfloat16)
    back_right = bdot("tjc,jic->tij", value_grad, sampled[3]).astype(jnp.bfloat16)
    second = mp_exchange(jnp.stack([outer, back_left, back_right], axis=1))
    mixed_rows, rows_left, rows_right = second[:, 0], second[:, 1], second[:, 2]
    grad_five = bdot("tji,tjc->jic", mixed_rows, grad_rows) * scale
    grad_zero = bdot("tbr,tbc->brc", in_rows, rows_left) * scale
    grad_two = bdot("tbr,tbc->brc", in_rows, rows_right) * scale
    all_grads = jnp.stack([grad_zero, grad_one, grad_two, grad_three, grad_four, grad_five])
    sums = scatter_rows(jnp.stack([all_grads, all_grads * noise * spread]), groups)
    grad_avg = sums[0] / groups
    hess_avg = sums[1] / groups
    new_grad = BETA_GRAD * grad_state + (1.0 - BETA_GRAD) * grad_avg
    new_hess = (
        BETA_HESS * hess_state
        + (1.0 - BETA_HESS) * hess_avg
        + 0.5 * (1.0 - BETA_HESS) ** 2 * (hess_state - hess_avg) ** 2 / (hess_state + DELTA_DAMP)
    )
    new_mean = mean_state - STEP_RATE * (new_grad + DELTA_DAMP * mean_state) / (
        new_hess + DELTA_DAMP
    )
    return (new_mean, new_hess, new_grad)


def solution(mesh):
    n_dp, n_mp = mesh.shape["dp"], mesh.shape["mp"]
    n_x = 4 if n_mp % 4 == 0 else 1
    split = Mesh(mesh.devices.reshape(n_dp, n_mp // n_x, n_x), ("dp", "my", "mx"))
    mp = ("my", "mx")
    return jax.shard_map(
        per_device,
        mesh=split,
        in_specs=(
            P("dp", mp),
            P("dp", mp),
            P(None, mp, "dp", None),
            P(None, mp, "dp", None),
            P(None, mp, "dp", None),
            P("dp", None, mp, None, None),
        ),
        out_specs=(P(None, mp, "dp", None), P(None, mp, "dp", None), P(None, mp, "dp", None)),
        check_vma=False,
    )
```

```python
import jax
import jax.numpy as jnp
from jax import lax
from jax.sharding import PartitionSpec as P

LAMBDA_SIZE = 100.0
DELTA_DAMP = 0.001
BETA_GRAD = 0.9
BETA_HESS = 0.9
STEP_RATE = 1.0

REDUCE_MODE = "a2a"


def bdot(form, left, right):
    return jnp.einsum(form, left, right, preferred_element_type=jnp.float32)


def silu_slope(value):
    sigm = jax.nn.sigmoid(value)
    return sigm * (1.0 + value * (1.0 - sigm))


def gather_rows(stacked, groups):
    moved = jnp.moveaxis(stacked, 3, 0)
    full = lax.all_gather(moved, "dp", axis=0, tiled=True)
    return jnp.moveaxis(full, 0, 3)


def scatter_rows(stacked, groups):
    s, f, b, r, w = stacked.shape
    split = stacked.reshape(s, f, b, groups, r // groups, w)
    split = jnp.moveaxis(split, 3, 0)
    if REDUCE_MODE == "a2a":
        got = lax.all_to_all(split, "dp", split_axis=0, concat_axis=0, tiled=True)
        summed = jnp.sum(got, axis=0)
    else:
        summed = lax.psum_scatter(split, "dp", scatter_dimension=0, tiled=False)
    return summed


def roll_major(x, shift):
    n = x.shape[0]
    doubled = jnp.concatenate([x, x], axis=0)
    start = jnp.mod(-shift, n)
    return lax.dynamic_slice_in_dim(doubled, start, n, axis=0)


def mp_exchange(send):
    t, s, nb, b = send.shape
    n = lax.axis_size("mp")
    me = lax.axis_index("mp")
    chunks = jnp.moveaxis(send.reshape(t, s, n, nb // n, b), 2, 0)
    rolled = roll_major(chunks, -me)
    recv = [rolled[0]]
    for k in range(1, n):
        pairs = [(i, (i + k) % n) for i in range(n)]
        recv.append(lax.ppermute(rolled[k], "mp", pairs))
    recv = jnp.stack(recv)
    rev = recv[jnp.array([(-q) % n for q in range(n)])]
    out = roll_major(rev, me)
    out = jnp.transpose(out, (1, 2, 3, 0, 4))
    return out.reshape(t, s, nb // n, n * b)


def per_device(inputs, out_grad, mean_state, hess_state, grad_state, noise_draw):
    tokens = inputs.shape[0]
    local_blocks = mean_state.shape[1]
    width = mean_state.shape[3]
    groups = lax.axis_size("dp")
    scale = tokens ** (-0.5)
    full = gather_rows(jnp.stack([mean_state, hess_state]), groups)
    full_mean, full_hess = full[0], full[1]
    spread = jnp.sqrt(LAMBDA_SIZE * (full_hess + DELTA_DAMP))
    noise = noise_draw[0]
    sampled = (full_mean + noise / spread).astype(jnp.bfloat16)
    in_rows = inputs.reshape(tokens, local_blocks, width)
    grad_rows = out_grad.reshape(tokens, local_blocks, width)
    y_left = bdot("tbr,brc->tcb", in_rows, sampled[0]).astype(jnp.bfloat16)
    y_right = bdot("tbr,brc->tcb", in_rows, sampled[2]).astype(jnp.bfloat16)
    back_outer = bdot("tjc,jic->tij", grad_rows, sampled[5]).astype(jnp.bfloat16)
    first = mp_exchange(jnp.stack([y_left, y_right, back_outer], axis=1))
    perm_left, perm_right, back_hidden = first[:, 0], first[:, 1], first[:, 2]
    u_left = bdot("tji,jic->tjc", perm_left, sampled[1])
    u_right = bdot("tji,jic->tjc", perm_right, sampled[3])
    hidden = (jax.nn.silu(u_left) * u_right).astype(jnp.bfloat16)
    outer = bdot("tbr,brc->tcb", hidden, sampled[4]).astype(jnp.bfloat16)
    grad_four = bdot("tbr,tbc->brc", hidden, back_hidden) * scale
    d_hidden = bdot("tbc,brc->tbr", back_hidden, sampled[4])
    gate_grad = (d_hidden * u_right * silu_slope(u_left)).astype(jnp.bfloat16)
    value_grad = (d_hidden * jax.nn.silu(u_left)).astype(jnp.bfloat16)
    grad_one = bdot("tji,tjc->jic", perm_left, gate_grad) * scale
    grad_three = bdot("tji,tjc->jic", perm_right, value_grad) * scale
    back_left = bdot("tjc,jic->tij", gate_grad, sampled[1]).astype(jnp.bfloat16)
    back_right = bdot("tjc,jic->tij", value_grad, sampled[3]).astype(jnp.bfloat16)
    second = mp_exchange(jnp.stack([outer, back_left, back_right], axis=1))
    mixed_rows, rows_left, rows_right = second[:, 0], second[:, 1], second[:, 2]
    grad_five = bdot("tji,tjc->jic", mixed_rows, grad_rows) * scale
    grad_zero = bdot("tbr,tbc->brc", in_rows, rows_left) * scale
    grad_two = bdot("tbr,tbc->brc", in_rows, rows_right) * scale
    all_grads = jnp.stack([grad_zero, grad_one, grad_two, grad_three, grad_four, grad_five])
    sums = scatter_rows(jnp.stack([all_grads, all_grads * noise * spread]), groups)
    grad_avg = sums[0] / groups
    hess_avg = sums[1] / groups
    new_grad = BETA_GRAD * grad_state + (1.0 - BETA_GRAD) * grad_avg
    new_hess = (
        BETA_HESS * hess_state
        + (1.0 - BETA_HESS) * hess_avg
        + 0.5 * (1.0 - BETA_HESS) ** 2 * (hess_state - hess_avg) ** 2 / (hess_state + DELTA_DAMP)
    )
    new_mean = mean_state - STEP_RATE * (new_grad + DELTA_DAMP * mean_state) / (
        new_hess + DELTA_DAMP
    )
    return (new_mean, new_hess, new_grad)


def solution(mesh):
    return jax.shard_map(
        per_device,
        mesh=mesh,
        in_specs=(
            P("dp", "mp"),
            P("dp", "mp"),
            P(None, "mp", "dp", None),
            P(None, "mp", "dp", None),
            P(None, "mp", "dp", None),
            P("dp", None, "mp", None, None),
        ),
        out_specs=(P(None, "mp", "dp", None), P(None, "mp", "dp", None), P(None, "mp", "dp", None)),
        check_vma=False,
    )
```

```python
import jax
import jax.numpy as jnp
from jax import lax
from jax.sharding import PartitionSpec as P

LAMBDA_SIZE = 100.0
DELTA_DAMP = 0.001
BETA_GRAD = 0.9
BETA_HESS = 0.9
STEP_RATE = 1.0

REDUCE_MODE = "a2a"


def bdot(form, left, right):
    return jnp.einsum(form, left, right, preferred_element_type=jnp.float32)


def silu_slope(value):
    sigm = jax.nn.sigmoid(value)
    return sigm * (1.0 + value * (1.0 - sigm))


def gather_rows(stacked, groups):
    moved = jnp.moveaxis(stacked, 3, 0)
    copies = jnp.broadcast_to(moved[None], (groups,) + moved.shape)
    full = lax.all_to_all(copies, "dp", split_axis=0, concat_axis=0, tiled=True)
    full = full.reshape((groups * moved.shape[0],) + moved.shape[1:])
    return jnp.moveaxis(full, 0, 3)


def mp_exchange(send):
    t, s, nb, b = send.shape
    n = lax.axis_size("mp")
    parts = send.reshape(t, s, n, nb // n, b)
    parts = jnp.swapaxes(parts, 2, 3)
    got = lax.all_to_all(parts, "mp", split_axis=3, concat_axis=3, tiled=True)
    return got.reshape(t, s, nb // n, n * b)


def scatter_rows(stacked, groups):
    s, f, b, r, w = stacked.shape
    split = stacked.reshape(s, f, b, groups, r // groups, w)
    split = jnp.moveaxis(split, 3, 0)
    if REDUCE_MODE == "a2a":
        got = lax.all_to_all(split, "dp", split_axis=0, concat_axis=0, tiled=True)
        summed = jnp.sum(got, axis=0)
    else:
        summed = lax.psum_scatter(split, "dp", scatter_dimension=0, tiled=False)
    return summed


def per_device(inputs, out_grad, mean_state, hess_state, grad_state, noise_draw):
    tokens = inputs.shape[0]
    local_blocks = mean_state.shape[1]
    width = mean_state.shape[3]
    groups = lax.axis_size("dp")
    scale = tokens ** (-0.5)
    full = gather_rows(jnp.stack([mean_state, hess_state]), groups)
    full_mean, full_hess = full[0], full[1]
    spread = jnp.sqrt(LAMBDA_SIZE * (full_hess + DELTA_DAMP))
    noise = noise_draw[0]
    sampled = (full_mean + noise / spread).astype(jnp.bfloat16)
    in_rows = inputs.reshape(tokens, local_blocks, width)
    grad_rows = out_grad.reshape(tokens, local_blocks, width)
    y_left = bdot("tbr,brc->tcb", in_rows, sampled[0]).astype(jnp.bfloat16)
    y_right = bdot("tbr,brc->tcb", in_rows, sampled[2]).astype(jnp.bfloat16)
    back_outer = bdot("tjc,jic->tij", grad_rows, sampled[5]).astype(jnp.bfloat16)
    first = mp_exchange(jnp.stack([y_left, y_right, back_outer], axis=1))
    perm_left, perm_right, back_hidden = first[:, 0], first[:, 1], first[:, 2]
    u_left = bdot("tji,jic->tjc", perm_left, sampled[1])
    u_right = bdot("tji,jic->tjc", perm_right, sampled[3])
    hidden = (jax.nn.silu(u_left) * u_right).astype(jnp.bfloat16)
    outer = bdot("tbr,brc->tcb", hidden, sampled[4]).astype(jnp.bfloat16)
    grad_four = bdot("tbr,tbc->brc", hidden, back_hidden) * scale
    d_hidden = bdot("tbc,brc->tbr", back_hidden, sampled[4])
    gate_grad = (d_hidden * u_right * silu_slope(u_left)).astype(jnp.bfloat16)
    value_grad = (d_hidden * jax.nn.silu(u_left)).astype(jnp.bfloat16)
    grad_one = bdot("tji,tjc->jic", perm_left, gate_grad) * scale
    grad_three = bdot("tji,tjc->jic", perm_right, value_grad) * scale
    back_left = bdot("tjc,jic->tij", gate_grad, sampled[1]).astype(jnp.bfloat16)
    back_right = bdot("tjc,jic->tij", value_grad, sampled[3]).astype(jnp.bfloat16)
    second = mp_exchange(jnp.stack([outer, back_left, back_right], axis=1))
    mixed_rows, rows_left, rows_right = second[:, 0], second[:, 1], second[:, 2]
    grad_five = bdot("tji,tjc->jic", mixed_rows, grad_rows) * scale
    grad_zero = bdot("tbr,tbc->brc", in_rows, rows_left) * scale
    grad_two = bdot("tbr,tbc->brc", in_rows, rows_right) * scale
    all_grads = jnp.stack([grad_zero, grad_one, grad_two, grad_three, grad_four, grad_five])
    sums = scatter_rows(jnp.stack([all_grads, all_grads * noise * spread]), groups)
    grad_avg = sums[0] / groups
    hess_avg = sums[1] / groups
    new_grad = BETA_GRAD * grad_state + (1.0 - BETA_GRAD) * grad_avg
    new_hess = (
        BETA_HESS * hess_state
        + (1.0 - BETA_HESS) * hess_avg
        + 0.5 * (1.0 - BETA_HESS) ** 2 * (hess_state - hess_avg) ** 2 / (hess_state + DELTA_DAMP)
    )
    new_mean = mean_state - STEP_RATE * (new_grad + DELTA_DAMP * mean_state) / (
        new_hess + DELTA_DAMP
    )
    return (new_mean, new_hess, new_grad)


def solution(mesh):
    return jax.shard_map(
        per_device,
        mesh=mesh,
        in_specs=(
            P("dp", "mp"),
            P("dp", "mp"),
            P(None, "mp", "dp", None),
            P(None, "mp", "dp", None),
            P(None, "mp", "dp", None),
            P("dp", None, "mp", None, None),
        ),
        out_specs=(P(None, "mp", "dp", None), P(None, "mp", "dp", None), P(None, "mp", "dp", None)),
        check_vma=False,
    )
```

```python
import jax
import jax.numpy as jnp
from jax import lax
from jax.experimental import pallas as pl
from jax.experimental.pallas import tpu as pltpu
from jax.sharding import PartitionSpec as P

LAMBDA_SIZE = 100.0
DELTA_DAMP = 0.001
BETA_GRAD = 0.9
BETA_HESS = 0.9
STEP_RATE = 1.0

REDUCE_MODE = "a2a"


def bdot(form, left, right):
    return jnp.einsum(form, left, right, preferred_element_type=jnp.float32)


def silu_slope(value):
    sigm = jax.nn.sigmoid(value)
    return sigm * (1.0 + value * (1.0 - sigm))


def gather_rows(stacked, groups):
    moved = jnp.moveaxis(stacked, 3, 0)
    full = lax.all_gather(moved, "dp", axis=0, tiled=True)
    return jnp.moveaxis(full, 0, 3)


def scatter_rows(stacked, groups):
    s, f, b, r, w = stacked.shape
    split = stacked.reshape(s, f, b, groups, r // groups, w)
    split = jnp.moveaxis(split, 3, 0)
    if REDUCE_MODE == "a2a":
        got = lax.all_to_all(split, "dp", split_axis=0, concat_axis=0, tiled=True)
        summed = jnp.sum(got, axis=0)
    else:
        summed = lax.psum_scatter(split, "dp", scatter_dimension=0, tiled=False)
    return summed


TOKEN_BLOCK = 512


def nt_dot(a, b):
    return lax.dot_general(a, b, (((1,), (1,)), ((), ())), preferred_element_type=jnp.float32)


def grads_kernel(x_ref, c_ref, first_ref, second_ref, h_ref, gl_ref, gr_ref, noise_ref, spread_ref,
                 out_ref, acc_ref, *, scale):
    step = pl.program_id(0)

    @pl.when(step == 0)
    def _():
        acc_ref[...] = jnp.zeros_like(acc_ref)

    for b in range(acc_ref.shape[1]):
        pairs = (
            (x_ref[b], second_ref[1, b]),
            (first_ref[0, b], gl_ref[b]),
            (x_ref[b], second_ref[2, b]),
            (first_ref[1, b], gr_ref[b]),
            (h_ref[b], first_ref[2, b]),
            (second_ref[0, b], c_ref[b]),
        )
        for f, (lhs, rhs) in enumerate(pairs):
            acc_ref[f, b] += nt_dot(lhs, rhs)

    @pl.when(step == pl.num_programs(0) - 1)
    def _():
        grads = acc_ref[...] * scale
        out_ref[0] = grads
        out_ref[1] = grads * noise_ref[...] * spread_ref[...]


def grads_and_curvature(x_t, c_t, first_t, second_t, h_t, gl_t, gr_t, noise, spread, scale):
    nb, width, tokens = x_t.shape
    tb = min(TOKEN_BLOCK, tokens)
    act = pl.BlockSpec((nb, width, tb), lambda i: (0, 0, i))
    trio = pl.BlockSpec((3, nb, width, tb), lambda i: (0, 0, 0, i))
    whole = pl.BlockSpec(noise.shape, lambda i: (0, 0, 0, 0))
    return pl.pallas_call(
        lambda *refs: grads_kernel(*refs, scale=scale),
        grid=(tokens // tb,),
        in_specs=[act, act, trio, trio, act, act, act, whole, whole],
        out_specs=pl.BlockSpec((2,) + noise.shape, lambda i: (0, 0, 0, 0, 0)),
        out_shape=jax.ShapeDtypeStruct((2,) + noise.shape, jnp.float32),
        scratch_shapes=[pltpu.VMEM(noise.shape, jnp.float32)],
        compiler_params=pltpu.CompilerParams(dimension_semantics=("arbitrary",)),
    )(x_t, c_t, first_t, second_t, h_t, gl_t, gr_t, noise, spread)


def per_device(inputs, out_grad, mean_state, hess_state, grad_state, noise_draw):
    tokens = inputs.shape[0]
    local_blocks = mean_state.shape[1]
    width = mean_state.shape[3]
    groups = lax.axis_size("dp")
    scale = tokens ** (-0.5)
    full = gather_rows(jnp.stack([mean_state, hess_state]), groups)
    full_mean, full_hess = full[0], full[1]
    spread = jnp.sqrt(LAMBDA_SIZE * (full_hess + DELTA_DAMP))
    noise = noise_draw[0]
    sampled = (full_mean + noise / spread).astype(jnp.bfloat16)
    in_rows = inputs.reshape(tokens, local_blocks, width)
    grad_rows = out_grad.reshape(tokens, local_blocks, width)
    y_left = bdot("tbr,brc->tcb", in_rows, sampled[0]).astype(jnp.bfloat16)
    y_right = bdot("tbr,brc->tcb", in_rows, sampled[2]).astype(jnp.bfloat16)
    back_outer = bdot("tjc,jic->tij", grad_rows, sampled[5]).astype(jnp.bfloat16)
    first = lax.all_to_all(
        jnp.stack([y_left, y_right, back_outer], axis=1), "mp", split_axis=2, concat_axis=3, tiled=True
    )
    perm_left, perm_right, back_hidden = first[:, 0], first[:, 1], first[:, 2]
    u_left = bdot("tji,jic->tjc", perm_left, sampled[1])
    u_right = bdot("tji,jic->tjc", perm_right, sampled[3])
    hidden = (jax.nn.silu(u_left) * u_right).astype(jnp.bfloat16)
    outer = bdot("tbr,brc->tcb", hidden, sampled[4]).astype(jnp.bfloat16)
    d_hidden = bdot("tbc,brc->tbr", back_hidden, sampled[4])
    gate_grad = (d_hidden * u_right * silu_slope(u_left)).astype(jnp.bfloat16)
    value_grad = (d_hidden * jax.nn.silu(u_left)).astype(jnp.bfloat16)
    back_left = bdot("tjc,jic->tij", gate_grad, sampled[1]).astype(jnp.bfloat16)
    back_right = bdot("tjc,jic->tij", value_grad, sampled[3]).astype(jnp.bfloat16)
    second = lax.all_to_all(
        jnp.stack([outer, back_left, back_right], axis=1), "mp", split_axis=2, concat_axis=3, tiled=True
    )
    token_minor = lambda a: jnp.moveaxis(a, 0, -1)
    stacked = grads_and_curvature(
        token_minor(in_rows), token_minor(grad_rows), token_minor(first), token_minor(second),
        token_minor(hidden), token_minor(gate_grad), token_minor(value_grad), noise, spread, scale,
    )
    sums = scatter_rows(stacked, groups)
    grad_avg = sums[0] / groups
    hess_avg = sums[1] / groups
    new_grad = BETA_GRAD * grad_state + (1.0 - BETA_GRAD) * grad_avg
    new_hess = (
        BETA_HESS * hess_state
        + (1.0 - BETA_HESS) * hess_avg
        + 0.5 * (1.0 - BETA_HESS) ** 2 * (hess_state - hess_avg) ** 2 / (hess_state + DELTA_DAMP)
    )
    new_mean = mean_state - STEP_RATE * (new_grad + DELTA_DAMP * mean_state) / (
        new_hess + DELTA_DAMP
    )
    return (new_mean, new_hess, new_grad)


def solution(mesh):
    return jax.shard_map(
        per_device,
        mesh=mesh,
        in_specs=(
            P("dp", "mp"),
            P("dp", "mp"),
            P(None, "mp", "dp", None),
            P(None, "mp", "dp", None),
            P(None, "mp", "dp", None),
            P("dp", None, "mp", None, None),
        ),
        out_specs=(P(None, "mp", "dp", None), P(None, "mp", "dp", None), P(None, "mp", "dp", None)),
        check_vma=False,
    )
```

```python
import jax
import jax.numpy as jnp
from jax import lax
from jax.experimental import pallas as pl
from jax.experimental.pallas import tpu as pltpu
from jax.sharding import PartitionSpec as P

LAMBDA_SIZE = 100.0
DELTA_DAMP = 0.001
BETA_GRAD = 0.9
BETA_HESS = 0.9
STEP_RATE = 1.0

REDUCE_MODE = "a2a"


def bdot(form, left, right):
    return jnp.einsum(form, left, right, preferred_element_type=jnp.float32)


def silu_slope(value):
    sigm = jax.nn.sigmoid(value)
    return sigm * (1.0 + value * (1.0 - sigm))


def gather_rows(stacked, groups):
    moved = jnp.moveaxis(stacked, 3, 0)
    full = lax.all_gather(moved, "dp", axis=0, tiled=True)
    return jnp.moveaxis(full, 0, 3)


def scatter_rows(stacked, groups):
    s, f, b, r, w = stacked.shape
    split = stacked.reshape(s, f, b, groups, r // groups, w)
    split = jnp.moveaxis(split, 3, 0)
    if REDUCE_MODE == "a2a":
        got = lax.all_to_all(split, "dp", split_axis=0, concat_axis=0, tiled=True)
        summed = jnp.sum(got, axis=0)
    else:
        summed = lax.psum_scatter(split, "dp", scatter_dimension=0, tiled=False)
    return summed


TOKEN_BLOCK = 1024


def nn_dot(a, b):
    return lax.dot_general(a, b, (((1,), (0,)), ((), ())), preferred_element_type=jnp.float32)


def grads_kernel(x_ref, c_ref, first_ref, second_ref, h_ref, gl_ref, gr_ref, noise_ref, spread_ref,
                 out_ref, acc_ref, *, scale):
    step = pl.program_id(0)
    nb, width = acc_ref.shape[1], acc_ref.shape[2]

    @pl.when(step == 0)
    def _():
        acc_ref[...] = jnp.zeros_like(acc_ref)

    for b in range(nb):
        cols = slice(b * width, (b + 1) * width)
        pairs = (
            (second_ref[1, b], x_ref[:, cols]),
            (first_ref[0, b], gl_ref[:, cols]),
            (second_ref[2, b], x_ref[:, cols]),
            (first_ref[1, b], gr_ref[:, cols]),
            (first_ref[2, b], h_ref[:, cols]),
            (second_ref[0, b], c_ref[:, cols]),
        )
        for f, (lhs, rhs) in enumerate(pairs):
            acc_ref[f, b] += nn_dot(lhs, rhs)

    @pl.when(step == pl.num_programs(0) - 1)
    def _():
        for f in range(acc_ref.shape[0]):
            for b in range(nb):
                grad = acc_ref[f, b]
                if f in (0, 2, 4):
                    grad = grad.T
                grad = grad * scale
                out_ref[0, f, b] = grad
                out_ref[1, f, b] = grad * noise_ref[f, b] * spread_ref[f, b]


def grads_and_curvature(x, c, first_t, second_t, h, gl, gr, noise, spread, scale):
    tokens, feats = x.shape
    nb, width = first_t.shape[1], first_t.shape[2]
    tb = min(TOKEN_BLOCK, tokens)
    act = pl.BlockSpec((tb, feats), lambda i: (i, 0))
    trio = pl.BlockSpec((3, nb, width, tb), lambda i: (0, 0, 0, i))
    whole = pl.BlockSpec(noise.shape, lambda i: (0, 0, 0, 0))
    return pl.pallas_call(
        lambda *refs: grads_kernel(*refs, scale=scale),
        grid=(tokens // tb,),
        in_specs=[act, act, trio, trio, act, act, act, whole, whole],
        out_specs=pl.BlockSpec((2,) + noise.shape, lambda i: (0, 0, 0, 0, 0)),
        out_shape=jax.ShapeDtypeStruct((2,) + noise.shape, jnp.float32),
        scratch_shapes=[pltpu.VMEM(noise.shape, jnp.float32)],
        compiler_params=pltpu.CompilerParams(dimension_semantics=("arbitrary",)),
    )(x, c, first_t, second_t, h, gl, gr, noise, spread)


def per_device(inputs, out_grad, mean_state, hess_state, grad_state, noise_draw):
    tokens = inputs.shape[0]
    local_blocks = mean_state.shape[1]
    width = mean_state.shape[3]
    groups = lax.axis_size("dp")
    scale = tokens ** (-0.5)
    full = gather_rows(jnp.stack([mean_state, hess_state]), groups)
    full_mean, full_hess = full[0], full[1]
    spread = jnp.sqrt(LAMBDA_SIZE * (full_hess + DELTA_DAMP))
    noise = noise_draw[0]
    sampled = (full_mean + noise / spread).astype(jnp.bfloat16)
    in_rows = inputs.reshape(tokens, local_blocks, width)
    grad_rows = out_grad.reshape(tokens, local_blocks, width)
    y_left = bdot("tbr,brc->tcb", in_rows, sampled[0]).astype(jnp.bfloat16)
    y_right = bdot("tbr,brc->tcb", in_rows, sampled[2]).astype(jnp.bfloat16)
    back_outer = bdot("tjc,jic->tij", grad_rows, sampled[5]).astype(jnp.bfloat16)
    first = lax.all_to_all(
        jnp.stack([y_left, y_right, back_outer], axis=1), "mp", split_axis=2, concat_axis=3, tiled=True
    )
    perm_left, perm_right, back_hidden = first[:, 0], first[:, 1], first[:, 2]
    u_left = bdot("tji,jic->tjc", perm_left, sampled[1])
    u_right = bdot("tji,jic->tjc", perm_right, sampled[3])
    hidden = (jax.nn.silu(u_left) * u_right).astype(jnp.bfloat16)
    outer = bdot("tbr,brc->tcb", hidden, sampled[4]).astype(jnp.bfloat16)
    d_hidden = bdot("tbc,brc->tbr", back_hidden, sampled[4])
    gate_grad = (d_hidden * u_right * silu_slope(u_left)).astype(jnp.bfloat16)
    value_grad = (d_hidden * jax.nn.silu(u_left)).astype(jnp.bfloat16)
    back_left = bdot("tjc,jic->tij", gate_grad, sampled[1]).astype(jnp.bfloat16)
    back_right = bdot("tjc,jic->tij", value_grad, sampled[3]).astype(jnp.bfloat16)
    second = lax.all_to_all(
        jnp.stack([outer, back_left, back_right], axis=1), "mp", split_axis=2, concat_axis=3, tiled=True
    )
    token_minor = lambda a: jnp.moveaxis(a, 0, -1)
    flat = lambda a: a.reshape(tokens, -1)
    stacked = grads_and_curvature(
        inputs, out_grad, token_minor(first), token_minor(second),
        flat(hidden), flat(gate_grad), flat(value_grad), noise, spread, scale,
    )
    sums = scatter_rows(stacked, groups)
    grad_avg = sums[0] / groups
    hess_avg = sums[1] / groups
    new_grad = BETA_GRAD * grad_state + (1.0 - BETA_GRAD) * grad_avg
    new_hess = (
        BETA_HESS * hess_state
        + (1.0 - BETA_HESS) * hess_avg
        + 0.5 * (1.0 - BETA_HESS) ** 2 * (hess_state - hess_avg) ** 2 / (hess_state + DELTA_DAMP)
    )
    new_mean = mean_state - STEP_RATE * (new_grad + DELTA_DAMP * mean_state) / (
        new_hess + DELTA_DAMP
    )
    return (new_mean, new_hess, new_grad)


def solution(mesh):
    return jax.shard_map(
        per_device,
        mesh=mesh,
        in_specs=(
            P("dp", "mp"),
            P("dp", "mp"),
            P(None, "mp", "dp", None),
            P(None, "mp", "dp", None),
            P(None, "mp", "dp", None),
            P("dp", None, "mp", None, None),
        ),
        out_specs=(P(None, "mp", "dp", None), P(None, "mp", "dp", None), P(None, "mp", "dp", None)),
        check_vma=False,
    )
```

```python
import jax
import jax.numpy as jnp
from jax import lax
from jax.experimental import pallas as pl
from jax.experimental.pallas import tpu as pltpu
from jax.sharding import PartitionSpec as P

LAMBDA_SIZE = 100.0
DELTA_DAMP = 0.001
BETA_GRAD = 0.9
BETA_HESS = 0.9
STEP_RATE = 1.0

REDUCE_MODE = "a2a"


def bdot(form, left, right):
    return jnp.einsum(form, left, right, preferred_element_type=jnp.float32)


def silu_slope(value):
    sigm = jax.nn.sigmoid(value)
    return sigm * (1.0 + value * (1.0 - sigm))


def gather_rows(stacked, groups):
    moved = jnp.moveaxis(stacked, 3, 0)
    full = lax.all_gather(moved, "dp", axis=0, tiled=True)
    return jnp.moveaxis(full, 0, 3)


def scatter_rows(stacked, groups):
    s, f, b, r, w = stacked.shape
    split = stacked.reshape(s, f, b, groups, r // groups, w)
    split = jnp.moveaxis(split, 3, 0)
    if REDUCE_MODE == "a2a":
        got = lax.all_to_all(split, "dp", split_axis=0, concat_axis=0, tiled=True)
        summed = jnp.sum(got, axis=0)
    else:
        summed = lax.psum_scatter(split, "dp", scatter_dimension=0, tiled=False)
    return summed


TOKEN_BLOCK = 1024


def nn_dot(a, b):
    return lax.dot_general(a, b, (((1,), (0,)), ((), ())), preferred_element_type=jnp.float32)


def grads_kernel(minor_ref, major_ref, noise_ref, spread_ref, out_ref, acc_ref, *, scale, pairs, flips):
    step = pl.program_id(0)
    nb, width = acc_ref.shape[1], acc_ref.shape[2]

    @pl.when(step == 0)
    def _():
        acc_ref[...] = jnp.zeros_like(acc_ref)

    for b in range(nb):
        cols = slice(b * width, (b + 1) * width)
        for f, (lhs, rhs) in enumerate(pairs):
            acc_ref[f, b] += nn_dot(minor_ref[lhs, b], major_ref[rhs, :, cols])

    @pl.when(step == pl.num_programs(0) - 1)
    def _():
        for f in range(acc_ref.shape[0]):
            for b in range(nb):
                grad = acc_ref[f, b]
                if flips[f]:
                    grad = grad.T
                grad = grad * scale
                out_ref[0, f, b] = grad
                out_ref[1, f, b] = grad * noise_ref[f, b] * spread_ref[f, b]


def grads_and_curvature(minor, major, noise, spread, scale, pairs, flips):
    n_minor, nb, width, tokens = minor.shape
    n_major, feats = major.shape[0], major.shape[2]
    tb = min(TOKEN_BLOCK, tokens)
    shape = (len(pairs), nb, width, width)
    whole = pl.BlockSpec(shape, lambda i: (0, 0, 0, 0))
    return pl.pallas_call(
        lambda *refs: grads_kernel(*refs, scale=scale, pairs=pairs, flips=flips),
        grid=(tokens // tb,),
        in_specs=[
            pl.BlockSpec((n_minor, nb, width, tb), lambda i: (0, 0, 0, i)),
            pl.BlockSpec((n_major, tb, feats), lambda i: (0, i, 0)),
            whole,
            whole,
        ],
        out_specs=pl.BlockSpec((2,) + shape, lambda i: (0, 0, 0, 0, 0)),
        out_shape=jax.ShapeDtypeStruct((2,) + shape, jnp.float32),
        scratch_shapes=[pltpu.VMEM(shape, jnp.float32)],
        compiler_params=pltpu.CompilerParams(dimension_semantics=("arbitrary",)),
    )(minor, major, noise, spread)


def per_device(inputs, out_grad, mean_state, hess_state, grad_state, noise_draw):
    tokens = inputs.shape[0]
    local_blocks = mean_state.shape[1]
    width = mean_state.shape[3]
    groups = lax.axis_size("dp")
    scale = tokens ** (-0.5)
    full = gather_rows(jnp.stack([mean_state, hess_state]), groups)
    full_mean, full_hess = full[0], full[1]
    spread = jnp.sqrt(LAMBDA_SIZE * (full_hess + DELTA_DAMP))
    noise = noise_draw[0]
    sampled = (full_mean + noise / spread).astype(jnp.bfloat16)
    in_rows = inputs.reshape(tokens, local_blocks, width)
    grad_rows = out_grad.reshape(tokens, local_blocks, width)
    y_left = bdot("tbr,brc->tcb", in_rows, sampled[0]).astype(jnp.bfloat16)
    y_right = bdot("tbr,brc->tcb", in_rows, sampled[2]).astype(jnp.bfloat16)
    back_outer = bdot("tjc,jic->tij", grad_rows, sampled[5]).astype(jnp.bfloat16)
    first = lax.all_to_all(
        jnp.stack([y_left, y_right, back_outer], axis=1), "mp", split_axis=2, concat_axis=3, tiled=True
    )
    perm_left, perm_right, back_hidden = first[:, 0], first[:, 1], first[:, 2]
    u_left = bdot("tji,jic->tjc", perm_left, sampled[1])
    u_right = bdot("tji,jic->tjc", perm_right, sampled[3])
    hidden = (jax.nn.silu(u_left) * u_right).astype(jnp.bfloat16)
    outer = bdot("tbr,brc->tcb", hidden, sampled[4]).astype(jnp.bfloat16)
    d_hidden = bdot("tbc,brc->tbr", back_hidden, sampled[4])
    gate_grad = (d_hidden * u_right * silu_slope(u_left)).astype(jnp.bfloat16)
    value_grad = (d_hidden * jax.nn.silu(u_left)).astype(jnp.bfloat16)
    back_left = bdot("tjc,jic->tij", gate_grad, sampled[1]).astype(jnp.bfloat16)
    back_right = bdot("tjc,jic->tij", value_grad, sampled[3]).astype(jnp.bfloat16)
    token_minor = lambda a: jnp.moveaxis(a, 0, -1)
    flat = lambda a: a.reshape(tokens, -1)
    early = grads_and_curvature(
        token_minor(first), jnp.stack([flat(gate_grad), flat(value_grad), flat(hidden)]),
        noise[jnp.array([1, 3, 4])], spread[jnp.array([1, 3, 4])], scale,
        pairs=((0, 0), (1, 1), (2, 2)), flips=(False, False, True),
    )
    early_sums = scatter_rows(early, groups)
    second = lax.all_to_all(
        jnp.stack([outer, back_left, back_right], axis=1), "mp", split_axis=2, concat_axis=3, tiled=True
    )
    late = grads_and_curvature(
        token_minor(second), jnp.stack([inputs, out_grad]),
        noise[jnp.array([0, 2, 5])], spread[jnp.array([0, 2, 5])], scale,
        pairs=((1, 0), (2, 0), (0, 1)), flips=(True, True, False),
    )
    late_sums = scatter_rows(late, groups)
    order = jnp.array([0, 3, 1, 4, 5, 2])
    sums = jnp.concatenate([late_sums, early_sums], axis=1)[:, order]
    grad_avg = sums[0] / groups
    hess_avg = sums[1] / groups
    new_grad = BETA_GRAD * grad_state + (1.0 - BETA_GRAD) * grad_avg
    new_hess = (
        BETA_HESS * hess_state
        + (1.0 - BETA_HESS) * hess_avg
        + 0.5 * (1.0 - BETA_HESS) ** 2 * (hess_state - hess_avg) ** 2 / (hess_state + DELTA_DAMP)
    )
    new_mean = mean_state - STEP_RATE * (new_grad + DELTA_DAMP * mean_state) / (
        new_hess + DELTA_DAMP
    )
    return (new_mean, new_hess, new_grad)


def solution(mesh):
    return jax.shard_map(
        per_device,
        mesh=mesh,
        in_specs=(
            P("dp", "mp"),
            P("dp", "mp"),
            P(None, "mp", "dp", None),
            P(None, "mp", "dp", None),
            P(None, "mp", "dp", None),
            P("dp", None, "mp", None, None),
        ),
        out_specs=(P(None, "mp", "dp", None), P(None, "mp", "dp", None), P(None, "mp", "dp", None)),
        check_vma=False,
    )
```

```python
import functools

import jax
import jax.numpy as jnp
from jax import lax
from jax.experimental import pallas as pl
from jax.experimental.pallas import tpu as pltpu
from jax.sharding import PartitionSpec as P

LAMBDA_SIZE = 100.0
DELTA_DAMP = 0.001
BETA_GRAD = 0.9
BETA_HESS = 0.9
STEP_RATE = 1.0

REDUCE_MODE = "a2a"


def bdot(form, left, right):
    return jnp.einsum(form, left, right, preferred_element_type=jnp.float32)


def silu_slope(value):
    sigm = jax.nn.sigmoid(value)
    return sigm * (1.0 + value * (1.0 - sigm))


def gather_rows(stacked, groups):
    moved = jnp.moveaxis(stacked, 3, 0)
    full = lax.all_gather(moved, "dp", axis=0, tiled=True)
    return jnp.moveaxis(full, 0, 3)


def scatter_rows(stacked, groups):
    s, f, b, r, w = stacked.shape
    split = stacked.reshape(s, f, b, groups, r // groups, w)
    split = jnp.moveaxis(split, 3, 0)
    if REDUCE_MODE == "a2a":
        got = lax.all_to_all(split, "dp", split_axis=0, concat_axis=0, tiled=True)
        summed = jnp.sum(got, axis=0)
    else:
        summed = lax.psum_scatter(split, "dp", scatter_dimension=0, tiled=False)
    return summed


TOKEN_BLOCK = 1024


def nn_dot(a, b):
    return lax.dot_general(a, b, (((1,), (0,)), ((), ())), preferred_element_type=jnp.float32)


def grads_kernel(*refs, scale, pairs, n_minor, n_major, carry):
    minor = refs[:n_minor]
    major = refs[n_minor:n_minor + n_major]
    noise_ref, spread_ref = refs[n_minor + n_major:n_minor + n_major + 2]
    rest = refs[n_minor + n_major + 2:]
    prev_ref = rest[0] if carry else None
    out_ref, acc_ref = rest[-2], rest[-1]
    step = pl.program_id(0)
    nb, width = acc_ref.shape[1], acc_ref.shape[2]

    @pl.when(step == 0)
    def _():
        acc_ref[...] = jnp.zeros_like(acc_ref)

    for b in range(nb):
        cols = slice(b * width, (b + 1) * width)
        for k, (f, lhs, rhs, flip) in enumerate(pairs):
            acc_ref[k, b] += nn_dot(minor[lhs][b], major[rhs][:, cols])

    @pl.when(step == pl.num_programs(0) - 1)
    def _():
        done = set()
        for k, (f, lhs, rhs, flip) in enumerate(pairs):
            done.add(f)
            for b in range(nb):
                grad = acc_ref[k, b]
                if flip:
                    grad = grad.T
                grad = grad * scale
                out_ref[0, f, b] = grad
                out_ref[1, f, b] = grad * noise_ref[f, b] * spread_ref[f, b]
        if carry:
            for f in range(noise_ref.shape[0]):
                if f not in done:
                    out_ref[:, f] = prev_ref[:, f]


def grads_and_curvature(minor, major, noise, spread, scale, pairs, prev=None):
    nb, width, tokens = minor[0].shape
    feats = major[0].shape[1]
    tb = min(TOKEN_BLOCK, tokens)
    whole4 = pl.BlockSpec(noise.shape, lambda i: (0, 0, 0, 0))
    whole5 = pl.BlockSpec((2,) + noise.shape, lambda i: (0, 0, 0, 0, 0))
    in_specs = (
        [pl.BlockSpec((nb, width, tb), lambda i: (0, 0, i))] * len(minor)
        + [pl.BlockSpec((tb, feats), lambda i: (i, 0))] * len(major)
        + [whole4, whole4]
    )
    operands = list(minor) + list(major) + [noise, spread]
    aliases = {}
    if prev is not None:
        in_specs.append(whole5)
        aliases = {len(operands): 0}
        operands.append(prev)
    kernel = functools.partial(
        grads_kernel, scale=scale, pairs=pairs, n_minor=len(minor), n_major=len(major),
        carry=prev is not None,
    )
    return pl.pallas_call(
        kernel,
        grid=(tokens // tb,),
        in_specs=in_specs,
        out_specs=whole5,
        out_shape=jax.ShapeDtypeStruct((2,) + noise.shape, jnp.float32),
        scratch_shapes=[pltpu.VMEM((len(pairs), nb, width, width), jnp.float32)],
        input_output_aliases=aliases,
        compiler_params=pltpu.CompilerParams(dimension_semantics=("arbitrary",)),
    )(*operands)


def per_device(inputs, out_grad, mean_state, hess_state, grad_state, noise_draw):
    tokens = inputs.shape[0]
    local_blocks = mean_state.shape[1]
    width = mean_state.shape[3]
    groups = lax.axis_size("dp")
    scale = tokens ** (-0.5)
    full = gather_rows(jnp.stack([mean_state, hess_state]), groups)
    full_mean, full_hess = full[0], full[1]
    spread = jnp.sqrt(LAMBDA_SIZE * (full_hess + DELTA_DAMP))
    noise = noise_draw[0]
    sampled = (full_mean + noise / spread).astype(jnp.bfloat16)
    in_rows = inputs.reshape(tokens, local_blocks, width)
    grad_rows = out_grad.reshape(tokens, local_blocks, width)
    y_left = bdot("tbr,brc->tcb", in_rows, sampled[0]).astype(jnp.bfloat16)
    y_right = bdot("tbr,brc->tcb", in_rows, sampled[2]).astype(jnp.bfloat16)
    back_outer = bdot("tjc,jic->tij", grad_rows, sampled[5]).astype(jnp.bfloat16)
    first = lax.all_to_all(
        jnp.stack([y_left, y_right, back_outer], axis=1), "mp", split_axis=2, concat_axis=3, tiled=True
    )
    perm_left, perm_right, back_hidden = first[:, 0], first[:, 1], first[:, 2]
    u_left = bdot("tji,jic->tjc", perm_left, sampled[1])
    u_right = bdot("tji,jic->tjc", perm_right, sampled[3])
    hidden = (jax.nn.silu(u_left) * u_right).astype(jnp.bfloat16)
    outer = bdot("tbr,brc->tcb", hidden, sampled[4]).astype(jnp.bfloat16)
    d_hidden = bdot("tbc,brc->tbr", back_hidden, sampled[4])
    gate_grad = (d_hidden * u_right * silu_slope(u_left)).astype(jnp.bfloat16)
    value_grad = (d_hidden * jax.nn.silu(u_left)).astype(jnp.bfloat16)
    back_left = bdot("tjc,jic->tij", gate_grad, sampled[1]).astype(jnp.bfloat16)
    back_right = bdot("tjc,jic->tij", value_grad, sampled[3]).astype(jnp.bfloat16)
    token_minor = lambda a: jnp.moveaxis(a, 0, -1)
    flat = lambda a: a.reshape(tokens, -1)
    first_t = token_minor(first)
    early = grads_and_curvature(
        [first_t[0], first_t[1], first_t[2]], [flat(gate_grad), flat(value_grad), flat(hidden)],
        noise, spread, scale, pairs=((1, 0, 0, False), (3, 1, 1, False), (4, 2, 2, True)),
    )
    second = lax.all_to_all(
        jnp.stack([outer, back_left, back_right], axis=1), "mp", split_axis=2, concat_axis=3, tiled=True
    )
    second_t = token_minor(second)
    stacked = grads_and_curvature(
        [second_t[0], second_t[1], second_t[2]], [inputs, out_grad],
        noise, spread, scale, pairs=((0, 1, 0, True), (2, 2, 0, True), (5, 0, 1, False)), prev=early,
    )
    sums = scatter_rows(stacked, groups)
    grad_avg = sums[0] / groups
    hess_avg = sums[1] / groups
    new_grad = BETA_GRAD * grad_state + (1.0 - BETA_GRAD) * grad_avg
    new_hess = (
        BETA_HESS * hess_state
        + (1.0 - BETA_HESS) * hess_avg
        + 0.5 * (1.0 - BETA_HESS) ** 2 * (hess_state - hess_avg) ** 2 / (hess_state + DELTA_DAMP)
    )
    new_mean = mean_state - STEP_RATE * (new_grad + DELTA_DAMP * mean_state) / (
        new_hess + DELTA_DAMP
    )
    return (new_mean, new_hess, new_grad)


def solution(mesh):
    return jax.shard_map(
        per_device,
        mesh=mesh,
        in_specs=(
            P("dp", "mp"),
            P("dp", "mp"),
            P(None, "mp", "dp", None),
            P(None, "mp", "dp", None),
            P(None, "mp", "dp", None),
            P("dp", None, "mp", None, None),
        ),
        out_specs=(P(None, "mp", "dp", None), P(None, "mp", "dp", None), P(None, "mp", "dp", None)),
        check_vma=False,
    )
```

```python
import functools

import jax
import jax.numpy as jnp
from jax import lax
from jax.experimental import pallas as pl
from jax.experimental.pallas import tpu as pltpu
from jax.sharding import PartitionSpec as P

LAMBDA_SIZE = 100.0
DELTA_DAMP = 0.001
BETA_GRAD = 0.9
BETA_HESS = 0.9
STEP_RATE = 1.0

REDUCE_MODE = "a2a"


def bdot(form, left, right):
    return jnp.einsum(form, left, right, preferred_element_type=jnp.float32)


def silu_slope(value):
    sigm = jax.nn.sigmoid(value)
    return sigm * (1.0 + value * (1.0 - sigm))


def gather_rows(stacked, groups):
    moved = jnp.moveaxis(stacked, 3, 0)
    full = lax.all_gather(moved, "dp", axis=0, tiled=True)
    return jnp.moveaxis(full, 0, 3)


def scatter_rows(stacked, groups):
    s, f, b, r, w = stacked.shape
    split = stacked.reshape(s, f, b, groups, r // groups, w)
    split = jnp.moveaxis(split, 3, 0)
    if REDUCE_MODE == "a2a":
        got = lax.all_to_all(split, "dp", split_axis=0, concat_axis=0, tiled=True)
        summed = jnp.sum(got, axis=0)
    else:
        summed = lax.psum_scatter(split, "dp", scatter_dimension=0, tiled=False)
    return summed


TOKEN_BLOCK = 1024


def nn_dot(a, b):
    return lax.dot_general(a, b, (((1,), (0,)), ((), ())), preferred_element_type=jnp.float32)


def grads_kernel(*refs, scale, pairs, n_minor, n_major, carry):
    minor = refs[:n_minor]
    major = refs[n_minor:n_minor + n_major]
    noise_ref, spread_ref = refs[n_minor + n_major:n_minor + n_major + 2]
    rest = refs[n_minor + n_major + 2:]
    prev_ref = rest[0] if carry else None
    out_ref, acc_ref = rest[-2], rest[-1]
    step = pl.program_id(0)
    nb, width = acc_ref.shape[1], acc_ref.shape[2]

    @pl.when(step == 0)
    def _():
        acc_ref[...] = jnp.zeros_like(acc_ref)

    for b in range(nb):
        cols = slice(b * width, (b + 1) * width)
        for k, (f, lhs, rhs, flip) in enumerate(pairs):
            acc_ref[k, b] += nn_dot(minor[0][lhs, b], major[rhs][:, cols])

    @pl.when(step == pl.num_programs(0) - 1)
    def _():
        done = set()
        for k, (f, lhs, rhs, flip) in enumerate(pairs):
            done.add(f)
            for b in range(nb):
                grad = acc_ref[k, b]
                if flip:
                    grad = grad.T
                grad = grad * scale
                out_ref[0, f, b] = grad
                out_ref[1, f, b] = grad * noise_ref[f, b] * spread_ref[f, b]
        if carry:
            for f in range(noise_ref.shape[0]):
                if f not in done:
                    out_ref[:, f] = prev_ref[:, f]


def grads_and_curvature(minor, major, noise, spread, scale, pairs, prev=None):
    n_minor, nb, width, tokens = minor.shape
    feats = major[0].shape[1]
    tb = min(TOKEN_BLOCK, tokens)
    whole4 = pl.BlockSpec(noise.shape, lambda i: (0, 0, 0, 0))
    whole5 = pl.BlockSpec((2,) + noise.shape, lambda i: (0, 0, 0, 0, 0))
    in_specs = (
        [pl.BlockSpec((n_minor, nb, width, tb), lambda i: (0, 0, 0, i))]
        + [pl.BlockSpec((tb, feats), lambda i: (i, 0))] * len(major)
        + [whole4, whole4]
    )
    operands = [minor] + list(major) + [noise, spread]
    aliases = {}
    if prev is not None:
        in_specs.append(whole5)
        aliases = {len(operands): 0}
        operands.append(prev)
    kernel = functools.partial(
        grads_kernel, scale=scale, pairs=pairs, n_minor=1, n_major=len(major),
        carry=prev is not None,
    )
    return pl.pallas_call(
        kernel,
        grid=(tokens // tb,),
        in_specs=in_specs,
        out_specs=whole5,
        out_shape=jax.ShapeDtypeStruct((2,) + noise.shape, jnp.float32),
        scratch_shapes=[pltpu.VMEM((len(pairs), nb, width, width), jnp.float32)],
        input_output_aliases=aliases,
        compiler_params=pltpu.CompilerParams(dimension_semantics=("arbitrary",)),
    )(*operands)


def per_device(inputs, out_grad, mean_state, hess_state, grad_state, noise_draw):
    tokens = inputs.shape[0]
    local_blocks = mean_state.shape[1]
    width = mean_state.shape[3]
    groups = lax.axis_size("dp")
    scale = tokens ** (-0.5)
    full = gather_rows(jnp.stack([mean_state, hess_state]), groups)
    full_mean, full_hess = full[0], full[1]
    spread = jnp.sqrt(LAMBDA_SIZE * (full_hess + DELTA_DAMP))
    noise = noise_draw[0]
    sampled = (full_mean + noise / spread).astype(jnp.bfloat16)
    in_rows = inputs.reshape(tokens, local_blocks, width)
    grad_rows = out_grad.reshape(tokens, local_blocks, width)
    y_left = bdot("tbr,brc->tcb", in_rows, sampled[0]).astype(jnp.bfloat16)
    y_right = bdot("tbr,brc->tcb", in_rows, sampled[2]).astype(jnp.bfloat16)
    back_outer = bdot("tjc,jic->tij", grad_rows, sampled[5]).astype(jnp.bfloat16)
    first = lax.all_to_all(
        jnp.stack([y_left, y_right, back_outer], axis=1), "mp", split_axis=2, concat_axis=3, tiled=True
    )
    perm_left, perm_right, back_hidden = first[:, 0], first[:, 1], first[:, 2]
    u_left = bdot("tji,jic->tjc", perm_left, sampled[1])
    u_right = bdot("tji,jic->tjc", perm_right, sampled[3])
    hidden = (jax.nn.silu(u_left) * u_right).astype(jnp.bfloat16)
    outer = bdot("tbr,brc->tcb", hidden, sampled[4]).astype(jnp.bfloat16)
    d_hidden = bdot("tbc,brc->tbr", back_hidden, sampled[4])
    gate_grad = (d_hidden * u_right * silu_slope(u_left)).astype(jnp.bfloat16)
    value_grad = (d_hidden * jax.nn.silu(u_left)).astype(jnp.bfloat16)
    back_left = bdot("tjc,jic->tij", gate_grad, sampled[1]).astype(jnp.bfloat16)
    back_right = bdot("tjc,jic->tij", value_grad, sampled[3]).astype(jnp.bfloat16)
    token_minor = lambda a: jnp.moveaxis(a, 0, -1)
    flat = lambda a: a.reshape(tokens, -1)
    first_t = token_minor(first)
    early = grads_and_curvature(
        first_t, [flat(gate_grad), flat(value_grad), flat(hidden)],
        noise, spread, scale, pairs=((1, 0, 0, False), (3, 1, 1, False), (4, 2, 2, True)),
    )
    second = lax.all_to_all(
        jnp.stack([outer, back_left, back_right], axis=1), "mp", split_axis=2, concat_axis=3, tiled=True
    )
    second_t = token_minor(second)
    stacked = grads_and_curvature(
        second_t, [inputs, out_grad],
        noise, spread, scale, pairs=((0, 1, 0, True), (2, 2, 0, True), (5, 0, 1, False)), prev=early,
    )
    sums = scatter_rows(stacked, groups)
    grad_avg = sums[0] / groups
    hess_avg = sums[1] / groups
    new_grad = BETA_GRAD * grad_state + (1.0 - BETA_GRAD) * grad_avg
    new_hess = (
        BETA_HESS * hess_state
        + (1.0 - BETA_HESS) * hess_avg
        + 0.5 * (1.0 - BETA_HESS) ** 2 * (hess_state - hess_avg) ** 2 / (hess_state + DELTA_DAMP)
    )
    new_mean = mean_state - STEP_RATE * (new_grad + DELTA_DAMP * mean_state) / (
        new_hess + DELTA_DAMP
    )
    return (new_mean, new_hess, new_grad)


def solution(mesh):
    return jax.shard_map(
        per_device,
        mesh=mesh,
        in_specs=(
            P("dp", "mp"),
            P("dp", "mp"),
            P(None, "mp", "dp", None),
            P(None, "mp", "dp", None),
            P(None, "mp", "dp", None),
            P("dp", None, "mp", None, None),
        ),
        out_specs=(P(None, "mp", "dp", None), P(None, "mp", "dp", None), P(None, "mp", "dp", None)),
        check_vma=False,
    )
```

```python
import functools

import jax
import jax.numpy as jnp
from jax import lax
from jax.experimental import pallas as pl
from jax.experimental.pallas import tpu as pltpu
from jax.sharding import PartitionSpec as P

LAMBDA_SIZE = 100.0
DELTA_DAMP = 0.001
BETA_GRAD = 0.9
BETA_HESS = 0.9
STEP_RATE = 1.0

REDUCE_MODE = "a2a"


def bdot(form, left, right):
    return jnp.einsum(form, left, right, preferred_element_type=jnp.float32)


def silu_slope(value):
    sigm = jax.nn.sigmoid(value)
    return sigm * (1.0 + value * (1.0 - sigm))


def gather_rows(stacked, groups):
    moved = jnp.moveaxis(stacked, 3, 0)
    full = lax.all_gather(moved, "dp", axis=0, tiled=True)
    return jnp.moveaxis(full, 0, 3)


def scatter_rows(stacked, groups):
    s, f, b, r, w = stacked.shape
    split = stacked.reshape(s, f, b, groups, r // groups, w)
    split = jnp.moveaxis(split, 3, 0)
    if REDUCE_MODE == "a2a":
        got = lax.all_to_all(split, "dp", split_axis=0, concat_axis=0, tiled=True)
        summed = jnp.sum(got, axis=0)
    else:
        summed = lax.psum_scatter(split, "dp", scatter_dimension=0, tiled=False)
    return summed


TOKEN_BLOCK = 1024


def nn_dot(a, b):
    return lax.dot_general(a, b, (((1,), (0,)), ((), ())), preferred_element_type=jnp.float32)


def grads_kernel(minor_ref, *refs, scale, prods, outs, n_major, carry):
    major = refs[:n_major]
    noise_ref, spread_ref = refs[n_major:n_major + 2]
    rest = refs[n_major + 2:]
    prev_ref = rest[0] if carry else None
    out_ref = rest[-1 - len(prods)]
    accs = rest[-len(prods):]
    step = pl.program_id(0)
    n_s, nb, width, tb = minor_ref.shape

    @pl.when(step == 0)
    def _():
        for acc in accs:
            acc[...] = jnp.zeros_like(acc)

    lhs = minor_ref[...].reshape(n_s * nb * width, tb)
    for k, (r0, rows, m) in enumerate(prods):
        accs[k][...] += nn_dot(lhs[r0:r0 + rows], major[m][...])

    @pl.when(step == pl.num_programs(0) - 1)
    def _():
        done = set()
        for f, k, r0, flip in outs:
            done.add(f)
            full = accs[k][...]
            for b in range(nb):
                grad = full[r0 + b * width:r0 + (b + 1) * width, b * width:(b + 1) * width]
                if flip:
                    grad = grad.T
                grad = grad * scale
                out_ref[0, f, b] = grad
                out_ref[1, f, b] = grad * noise_ref[f, b] * spread_ref[f, b]
        if carry:
            for f in range(noise_ref.shape[0]):
                if f not in done:
                    out_ref[:, f] = prev_ref[:, f]


def grads_and_curvature(minor, major, noise, spread, scale, prods, outs, prev=None):
    n_s, nb, width, tokens = minor.shape
    feats = major[0].shape[1]
    tb = min(TOKEN_BLOCK, tokens)
    whole4 = pl.BlockSpec(noise.shape, lambda i: (0, 0, 0, 0))
    whole5 = pl.BlockSpec((2,) + noise.shape, lambda i: (0, 0, 0, 0, 0))
    in_specs = (
        [pl.BlockSpec((n_s, nb, width, tb), lambda i: (0, 0, 0, i))]
        + [pl.BlockSpec((tb, feats), lambda i: (i, 0))] * len(major)
        + [whole4, whole4]
    )
    operands = [minor] + list(major) + [noise, spread]
    aliases = {}
    if prev is not None:
        in_specs.append(whole5)
        aliases = {len(operands): 0}
        operands.append(prev)
    kernel = functools.partial(
        grads_kernel, scale=scale, prods=prods, outs=outs, n_major=len(major), carry=prev is not None,
    )
    return pl.pallas_call(
        kernel,
        grid=(tokens // tb,),
        in_specs=in_specs,
        out_specs=whole5,
        out_shape=jax.ShapeDtypeStruct((2,) + noise.shape, jnp.float32),
        scratch_shapes=[pltpu.VMEM((rows, feats), jnp.float32) for _, rows, _ in prods],
        input_output_aliases=aliases,
        compiler_params=pltpu.CompilerParams(dimension_semantics=("arbitrary",)),
    )(*operands)


def per_device(inputs, out_grad, mean_state, hess_state, grad_state, noise_draw):
    tokens = inputs.shape[0]
    local_blocks = mean_state.shape[1]
    width = mean_state.shape[3]
    groups = lax.axis_size("dp")
    scale = tokens ** (-0.5)
    full = gather_rows(jnp.stack([mean_state, hess_state]), groups)
    full_mean, full_hess = full[0], full[1]
    spread = jnp.sqrt(LAMBDA_SIZE * (full_hess + DELTA_DAMP))
    noise = noise_draw[0]
    sampled = (full_mean + noise / spread).astype(jnp.bfloat16)
    in_rows = inputs.reshape(tokens, local_blocks, width)
    grad_rows = out_grad.reshape(tokens, local_blocks, width)
    y_left = bdot("tbr,brc->tcb", in_rows, sampled[0]).astype(jnp.bfloat16)
    y_right = bdot("tbr,brc->tcb", in_rows, sampled[2]).astype(jnp.bfloat16)
    back_outer = bdot("tjc,jic->tij", grad_rows, sampled[5]).astype(jnp.bfloat16)
    first = lax.all_to_all(
        jnp.stack([y_left, y_right, back_outer], axis=1), "mp", split_axis=2, concat_axis=3, tiled=True
    )
    perm_left, perm_right, back_hidden = first[:, 0], first[:, 1], first[:, 2]
    u_left = bdot("tji,jic->tjc", perm_left, sampled[1])
    u_right = bdot("tji,jic->tjc", perm_right, sampled[3])
    hidden = (jax.nn.silu(u_left) * u_right).astype(jnp.bfloat16)
    outer = bdot("tbr,brc->tcb", hidden, sampled[4]).astype(jnp.bfloat16)
    d_hidden = bdot("tbc,brc->tbr", back_hidden, sampled[4])
    gate_grad = (d_hidden * u_right * silu_slope(u_left)).astype(jnp.bfloat16)
    value_grad = (d_hidden * jax.nn.silu(u_left)).astype(jnp.bfloat16)
    back_left = bdot("tjc,jic->tij", gate_grad, sampled[1]).astype(jnp.bfloat16)
    back_right = bdot("tjc,jic->tij", value_grad, sampled[3]).astype(jnp.bfloat16)
    token_minor = lambda a: jnp.moveaxis(a, 0, -1)
    flat = lambda a: a.reshape(tokens, -1)
    first_t = token_minor(first)
    early = grads_and_curvature(
        first_t, [flat(gate_grad), flat(value_grad), flat(hidden)], noise, spread, scale,
        prods=((0, 128, 0), (128, 128, 1), (256, 128, 2)),
        outs=((1, 0, 0, False), (3, 1, 0, False), (4, 2, 0, True)),
    )
    second = lax.all_to_all(
        jnp.stack([outer, back_left, back_right], axis=1), "mp", split_axis=2, concat_axis=3, tiled=True
    )
    second_t = token_minor(second)
    stacked = grads_and_curvature(
        second_t, [inputs, out_grad], noise, spread, scale,
        prods=((128, 256, 0), (0, 128, 1)),
        outs=((0, 0, 0, True), (2, 0, 128, True), (5, 1, 0, False)), prev=early,
    )
    sums = scatter_rows(stacked, groups)
    grad_avg = sums[0] / groups
    hess_avg = sums[1] / groups
    new_grad = BETA_GRAD * grad_state + (1.0 - BETA_GRAD) * grad_avg
    new_hess = (
        BETA_HESS * hess_state
        + (1.0 - BETA_HESS) * hess_avg
        + 0.5 * (1.0 - BETA_HESS) ** 2 * (hess_state - hess_avg) ** 2 / (hess_state + DELTA_DAMP)
    )
    new_mean = mean_state - STEP_RATE * (new_grad + DELTA_DAMP * mean_state) / (
        new_hess + DELTA_DAMP
    )
    return (new_mean, new_hess, new_grad)


def solution(mesh):
    return jax.shard_map(
        per_device,
        mesh=mesh,
        in_specs=(
            P("dp", "mp"),
            P("dp", "mp"),
            P(None, "mp", "dp", None),
            P(None, "mp", "dp", None),
            P(None, "mp", "dp", None),
            P("dp", None, "mp", None, None),
        ),
        out_specs=(P(None, "mp", "dp", None), P(None, "mp", "dp", None), P(None, "mp", "dp", None)),
        check_vma=False,
    )
```

```python
import functools

import jax
import jax.numpy as jnp
from jax import lax
from jax.experimental import pallas as pl
from jax.experimental.pallas import tpu as pltpu
from jax.sharding import PartitionSpec as P

LAMBDA_SIZE = 100.0
DELTA_DAMP = 0.001
BETA_GRAD = 0.9
BETA_HESS = 0.9
STEP_RATE = 1.0

REDUCE_MODE = "a2a"


def bdot(form, left, right):
    return jnp.einsum(form, left, right, preferred_element_type=jnp.float32)


def silu_slope(value):
    sigm = jax.nn.sigmoid(value)
    return sigm * (1.0 + value * (1.0 - sigm))


def gather_rows(stacked, groups):
    moved = jnp.moveaxis(stacked, 3, 0)
    full = lax.all_gather(moved, "dp", axis=0, tiled=True)
    return jnp.moveaxis(full, 0, 3)


def scatter_rows(stacked, groups):
    s, f, b, r, w = stacked.shape
    split = stacked.reshape(s, f, b, groups, r // groups, w)
    split = jnp.moveaxis(split, 3, 0)
    if REDUCE_MODE == "a2a":
        got = lax.all_to_all(split, "dp", split_axis=0, concat_axis=0, tiled=True)
        summed = jnp.sum(got, axis=0)
    else:
        summed = lax.psum_scatter(split, "dp", scatter_dimension=0, tiled=False)
    return summed


TOKEN_BLOCK = 1024


def nn_dot(a, b):
    return lax.dot_general(a, b, (((1,), (0,)), ((), ())), preferred_element_type=jnp.float32)


def grads_kernel(minor_ref, *refs, scale, prods, outs, n_major):
    n_out = len(outs)
    major = refs[:n_major]
    noise_refs = refs[n_major:n_major + n_out]
    spread_refs = refs[n_major + n_out:n_major + 2 * n_out]
    out_ref = refs[n_major + 2 * n_out]
    accs = refs[n_major + 2 * n_out + 1:]
    step = pl.program_id(0)
    n_s, nb, width, tb = minor_ref.shape

    @pl.when(step == 0)
    def _():
        for acc in accs:
            acc[...] = jnp.zeros_like(acc)

    lhs = minor_ref[...].reshape(n_s * nb * width, tb)
    for k, (r0, rows, m) in enumerate(prods):
        accs[k][...] += nn_dot(lhs[r0:r0 + rows], major[m][...])

    @pl.when(step == pl.num_programs(0) - 1)
    def _():
        for q, (k, r0, flip) in enumerate(outs):
            full = accs[k][...]
            for b in range(nb):
                grad = full[r0 + b * width:r0 + (b + 1) * width, b * width:(b + 1) * width]
                if flip:
                    grad = grad.T
                grad = grad * scale
                out_ref[0, q, b] = grad
                out_ref[1, q, b] = grad * noise_refs[q][0, b] * spread_refs[q][0, b]


def grads_and_curvature(minor, major, noise, spread, scale, prods, outs, factors):
    n_s, nb, width, tokens = minor.shape
    feats = major[0].shape[1]
    tb = min(TOKEN_BLOCK, tokens)
    shape = (len(factors), nb, width, width)
    picks = [pl.BlockSpec((1, nb, width, width), lambda i, f=f: (f, 0, 0, 0)) for f in factors]
    in_specs = (
        [pl.BlockSpec((n_s, nb, width, tb), lambda i: (0, 0, 0, i))]
        + [pl.BlockSpec((tb, feats), lambda i: (i, 0))] * len(major)
        + picks + picks
    )
    operands = [minor] + list(major) + [noise] * len(factors) + [spread] * len(factors)
    kernel = functools.partial(grads_kernel, scale=scale, prods=prods, outs=outs, n_major=len(major))
    return pl.pallas_call(
        kernel,
        grid=(tokens // tb,),
        in_specs=in_specs,
        out_specs=pl.BlockSpec((2,) + shape, lambda i: (0, 0, 0, 0, 0)),
        out_shape=jax.ShapeDtypeStruct((2,) + shape, jnp.float32),
        scratch_shapes=[pltpu.VMEM((rows, feats), jnp.float32) for _, rows, _ in prods],
        compiler_params=pltpu.CompilerParams(dimension_semantics=("arbitrary",)),
    )(*operands)


def per_device(inputs, out_grad, mean_state, hess_state, grad_state, noise_draw):
    tokens = inputs.shape[0]
    local_blocks = mean_state.shape[1]
    width = mean_state.shape[3]
    groups = lax.axis_size("dp")
    scale = tokens ** (-0.5)
    full = gather_rows(jnp.stack([mean_state, hess_state]), groups)
    full_mean, full_hess = full[0], full[1]
    spread = jnp.sqrt(LAMBDA_SIZE * (full_hess + DELTA_DAMP))
    noise = noise_draw[0]
    sampled = (full_mean + noise / spread).astype(jnp.bfloat16)
    in_rows = inputs.reshape(tokens, local_blocks, width)
    grad_rows = out_grad.reshape(tokens, local_blocks, width)
    y_left = bdot("tbr,brc->tcb", in_rows, sampled[0]).astype(jnp.bfloat16)
    y_right = bdot("tbr,brc->tcb", in_rows, sampled[2]).astype(jnp.bfloat16)
    back_outer = bdot("tjc,jic->tij", grad_rows, sampled[5]).astype(jnp.bfloat16)
    first = lax.all_to_all(
        jnp.stack([y_left, y_right, back_outer], axis=1), "mp", split_axis=2, concat_axis=3, tiled=True
    )
    perm_left, perm_right, back_hidden = first[:, 0], first[:, 1], first[:, 2]
    u_left = bdot("tji,jic->tjc", perm_left, sampled[1])
    u_right = bdot("tji,jic->tjc", perm_right, sampled[3])
    hidden = (jax.nn.silu(u_left) * u_right).astype(jnp.bfloat16)
    outer = bdot("tbr,brc->tcb", hidden, sampled[4]).astype(jnp.bfloat16)
    d_hidden = bdot("tbc,brc->tbr", back_hidden, sampled[4])
    gate_grad = (d_hidden * u_right * silu_slope(u_left)).astype(jnp.bfloat16)
    value_grad = (d_hidden * jax.nn.silu(u_left)).astype(jnp.bfloat16)
    back_left = bdot("tjc,jic->tij", gate_grad, sampled[1]).astype(jnp.bfloat16)
    back_right = bdot("tjc,jic->tij", value_grad, sampled[3]).astype(jnp.bfloat16)
    token_minor = lambda a: jnp.moveaxis(a, 0, -1)
    flat = lambda a: a.reshape(tokens, -1)
    first_t = token_minor(first)
    early = grads_and_curvature(
        first_t, [flat(gate_grad), flat(value_grad), flat(hidden)], noise, spread, scale,
        prods=((0, 128, 0), (128, 128, 1), (256, 128, 2)),
        outs=((0, 0, False), (1, 0, False), (2, 0, True)), factors=(1, 3, 4),
    )
    second = lax.all_to_all(
        jnp.stack([outer, back_left, back_right], axis=1), "mp", split_axis=2, concat_axis=3, tiled=True
    )
    second_t = token_minor(second)
    late = grads_and_curvature(
        second_t, [inputs, out_grad], noise, spread, scale,
        prods=((128, 256, 0), (0, 128, 1)),
        outs=((0, 0, True), (0, 128, True), (1, 0, False)), factors=(0, 2, 5),
    )
    stacked = jnp.concatenate(
        [late[:, 0:1], early[:, 0:1], late[:, 1:2], early[:, 1:2], early[:, 2:3], late[:, 2:3]], axis=1
    )
    sums = scatter_rows(stacked, groups)
    grad_avg = sums[0] / groups
    hess_avg = sums[1] / groups
    new_grad = BETA_GRAD * grad_state + (1.0 - BETA_GRAD) * grad_avg
    new_hess = (
        BETA_HESS * hess_state
        + (1.0 - BETA_HESS) * hess_avg
        + 0.5 * (1.0 - BETA_HESS) ** 2 * (hess_state - hess_avg) ** 2 / (hess_state + DELTA_DAMP)
    )
    new_mean = mean_state - STEP_RATE * (new_grad + DELTA_DAMP * mean_state) / (
        new_hess + DELTA_DAMP
    )
    return (new_mean, new_hess, new_grad)


def solution(mesh):
    return jax.shard_map(
        per_device,
        mesh=mesh,
        in_specs=(
            P("dp", "mp"),
            P("dp", "mp"),
            P(None, "mp", "dp", None),
            P(None, "mp", "dp", None),
            P(None, "mp", "dp", None),
            P("dp", None, "mp", None, None),
        ),
        out_specs=(P(None, "mp", "dp", None), P(None, "mp", "dp", None), P(None, "mp", "dp", None)),
        check_vma=False,
    )
```

```python
import functools

import jax
import jax.numpy as jnp
from jax import lax
from jax.experimental import pallas as pl
from jax.experimental.pallas import tpu as pltpu
from jax.sharding import PartitionSpec as P

LAMBDA_SIZE = 100.0
DELTA_DAMP = 0.001
BETA_GRAD = 0.9
BETA_HESS = 0.9
STEP_RATE = 1.0

REDUCE_MODE = "a2a"


def bdot(form, left, right):
    return jnp.einsum(form, left, right, preferred_element_type=jnp.float32)


def silu_slope(value):
    sigm = jax.nn.sigmoid(value)
    return sigm * (1.0 + value * (1.0 - sigm))


def gather_rows(stacked, groups):
    moved = jnp.moveaxis(stacked, 3, 0)
    full = lax.all_gather(moved, "dp", axis=0, tiled=True)
    return jnp.moveaxis(full, 0, 3)


def scatter_rows(stacked, groups):
    s, f, b, r, w = stacked.shape
    split = stacked.reshape(s, f, b, groups, r // groups, w)
    split = jnp.moveaxis(split, 3, 0)
    if REDUCE_MODE == "a2a":
        dense = split.reshape(groups, -1, 128)
        got = lax.all_to_all(dense, "dp", split_axis=0, concat_axis=0, tiled=True)
        summed = jnp.sum(got, axis=0).reshape(split.shape[1:])
    else:
        summed = lax.psum_scatter(split, "dp", scatter_dimension=0, tiled=False)
    return summed


TOKEN_BLOCK = 1024


def nn_dot(a, b):
    return lax.dot_general(a, b, (((1,), (0,)), ((), ())), preferred_element_type=jnp.float32)


def grads_kernel(*refs, scale, pairs, n_minor, n_major, carry):
    minor = refs[:n_minor]
    major = refs[n_minor:n_minor + n_major]
    noise_ref, spread_ref = refs[n_minor + n_major:n_minor + n_major + 2]
    rest = refs[n_minor + n_major + 2:]
    prev_ref = rest[0] if carry else None
    out_ref, acc_ref = rest[-2], rest[-1]
    step = pl.program_id(0)
    nb, width = acc_ref.shape[1], acc_ref.shape[2]

    @pl.when(step == 0)
    def _():
        acc_ref[...] = jnp.zeros_like(acc_ref)

    for b in range(nb):
        cols = slice(b * width, (b + 1) * width)
        for k, (f, lhs, rhs, flip) in enumerate(pairs):
            acc_ref[k, b] += nn_dot(minor[0][lhs, b], major[rhs][:, cols])

    @pl.when(step == pl.num_programs(0) - 1)
    def _():
        done = set()
        for k, (f, lhs, rhs, flip) in enumerate(pairs):
            done.add(f)
            for b in range(nb):
                grad = acc_ref[k, b]
                if flip:
                    grad = grad.T
                grad = grad * scale
                out_ref[0, f, b] = grad
                out_ref[1, f, b] = grad * noise_ref[f, b] * spread_ref[f, b]
        if carry:
            for f in range(noise_ref.shape[0]):
                if f not in done:
                    out_ref[:, f] = prev_ref[:, f]


def grads_and_curvature(minor, major, noise, spread, scale, pairs, prev=None):
    n_minor, nb, width, tokens = minor.shape
    feats = major[0].shape[1]
    tb = min(TOKEN_BLOCK, tokens)
    whole4 = pl.BlockSpec(noise.shape, lambda i: (0, 0, 0, 0))
    whole5 = pl.BlockSpec((2,) + noise.shape, lambda i: (0, 0, 0, 0, 0))
    in_specs = (
        [pl.BlockSpec((n_minor, nb, width, tb), lambda i: (0, 0, 0, i))]
        + [pl.BlockSpec((tb, feats), lambda i: (i, 0))] * len(major)
        + [whole4, whole4]
    )
    operands = [minor] + list(major) + [noise, spread]
    aliases = {}
    if prev is not None:
        in_specs.append(whole5)
        aliases = {len(operands): 0}
        operands.append(prev)
    kernel = functools.partial(
        grads_kernel, scale=scale, pairs=pairs, n_minor=1, n_major=len(major),
        carry=prev is not None,
    )
    return pl.pallas_call(
        kernel,
        grid=(tokens // tb,),
        in_specs=in_specs,
        out_specs=whole5,
        out_shape=jax.ShapeDtypeStruct((2,) + noise.shape, jnp.float32),
        scratch_shapes=[pltpu.VMEM((len(pairs), nb, width, width), jnp.float32)],
        input_output_aliases=aliases,
        compiler_params=pltpu.CompilerParams(dimension_semantics=("arbitrary",)),
    )(*operands)


def per_device(inputs, out_grad, mean_state, hess_state, grad_state, noise_draw):
    tokens = inputs.shape[0]
    local_blocks = mean_state.shape[1]
    width = mean_state.shape[3]
    groups = lax.axis_size("dp")
    scale = tokens ** (-0.5)
    full = gather_rows(jnp.stack([mean_state, hess_state]), groups)
    full_mean, full_hess = full[0], full[1]
    spread = jnp.sqrt(LAMBDA_SIZE * (full_hess + DELTA_DAMP))
    noise = noise_draw[0]
    sampled = (full_mean + noise / spread).astype(jnp.bfloat16)
    in_rows = inputs.reshape(tokens, local_blocks, width)
    grad_rows = out_grad.reshape(tokens, local_blocks, width)
    y_left = bdot("tbr,brc->tcb", in_rows, sampled[0]).astype(jnp.bfloat16)
    y_right = bdot("tbr,brc->tcb", in_rows, sampled[2]).astype(jnp.bfloat16)
    back_outer = bdot("tjc,jic->tij", grad_rows, sampled[5]).astype(jnp.bfloat16)
    first = lax.all_to_all(
        jnp.stack([y_left, y_right, back_outer], axis=1), "mp", split_axis=2, concat_axis=3, tiled=True
    )
    perm_left, perm_right, back_hidden = first[:, 0], first[:, 1], first[:, 2]
    u_left = bdot("tji,jic->tjc", perm_left, sampled[1])
    u_right = bdot("tji,jic->tjc", perm_right, sampled[3])
    hidden = (jax.nn.silu(u_left) * u_right).astype(jnp.bfloat16)
    outer = bdot("tbr,brc->tcb", hidden, sampled[4]).astype(jnp.bfloat16)
    d_hidden = bdot("tbc,brc->tbr", back_hidden, sampled[4])
    gate_grad = (d_hidden * u_right * silu_slope(u_left)).astype(jnp.bfloat16)
    value_grad = (d_hidden * jax.nn.silu(u_left)).astype(jnp.bfloat16)
    back_left = bdot("tjc,jic->tij", gate_grad, sampled[1]).astype(jnp.bfloat16)
    back_right = bdot("tjc,jic->tij", value_grad, sampled[3]).astype(jnp.bfloat16)
    token_minor = lambda a: jnp.moveaxis(a, 0, -1)
    flat = lambda a: a.reshape(tokens, -1)
    first_t = token_minor(first)
    early = grads_and_curvature(
        first_t, [flat(gate_grad), flat(value_grad), flat(hidden)],
        noise, spread, scale, pairs=((1, 0, 0, False), (3, 1, 1, False), (4, 2, 2, True)),
    )
    second = lax.all_to_all(
        jnp.stack([outer, back_left, back_right], axis=1), "mp", split_axis=2, concat_axis=3, tiled=True
    )
    second_t = token_minor(second)
    stacked = grads_and_curvature(
        second_t, [inputs, out_grad],
        noise, spread, scale, pairs=((0, 1, 0, True), (2, 2, 0, True), (5, 0, 1, False)), prev=early,
    )
    sums = scatter_rows(stacked, groups)
    grad_avg = sums[0] / groups
    hess_avg = sums[1] / groups
    new_grad = BETA_GRAD * grad_state + (1.0 - BETA_GRAD) * grad_avg
    new_hess = (
        BETA_HESS * hess_state
        + (1.0 - BETA_HESS) * hess_avg
        + 0.5 * (1.0 - BETA_HESS) ** 2 * (hess_state - hess_avg) ** 2 / (hess_state + DELTA_DAMP)
    )
    new_mean = mean_state - STEP_RATE * (new_grad + DELTA_DAMP * mean_state) / (
        new_hess + DELTA_DAMP
    )
    return (new_mean, new_hess, new_grad)


def solution(mesh):
    return jax.shard_map(
        per_device,
        mesh=mesh,
        in_specs=(
            P("dp", "mp"),
            P("dp", "mp"),
            P(None, "mp", "dp", None),
            P(None, "mp", "dp", None),
            P(None, "mp", "dp", None),
            P("dp", None, "mp", None, None),
        ),
        out_specs=(P(None, "mp", "dp", None), P(None, "mp", "dp", None), P(None, "mp", "dp", None)),
        check_vma=False,
    )
```

```python
import functools

import jax
import jax.numpy as jnp
from jax import lax
from jax.experimental import pallas as pl
from jax.experimental.pallas import tpu as pltpu
from jax.sharding import PartitionSpec as P

LAMBDA_SIZE = 100.0
DELTA_DAMP = 0.001
BETA_GRAD = 0.9
BETA_HESS = 0.9
STEP_RATE = 1.0

REDUCE_MODE = "a2a"


def bdot(form, left, right):
    return jnp.einsum(form, left, right, preferred_element_type=jnp.float32)


def silu_slope(value):
    sigm = jax.nn.sigmoid(value)
    return sigm * (1.0 + value * (1.0 - sigm))


def gather_rows(stacked, groups):
    shape = stacked.shape
    full = lax.all_gather(stacked.reshape(-1, 128), "dp", axis=0, tiled=True)
    full = jnp.moveaxis(full.reshape((groups,) + shape), 0, 3)
    return full.reshape(shape[:3] + (groups * shape[3], shape[4]))


def scatter_rows(stacked, groups):
    s, f, b, r, w = stacked.shape
    split = stacked.reshape(s, f, b, groups, r // groups, w)
    split = jnp.moveaxis(split, 3, 0)
    if REDUCE_MODE == "a2a":
        dense = split.reshape(groups, -1, 128)
        got = lax.all_to_all(dense, "dp", split_axis=0, concat_axis=0, tiled=True)
        summed = jnp.sum(got, axis=0).reshape(split.shape[1:])
    else:
        summed = lax.psum_scatter(split, "dp", scatter_dimension=0, tiled=False)
    return summed


TOKEN_BLOCK = 1024


def nn_dot(a, b):
    return lax.dot_general(a, b, (((1,), (0,)), ((), ())), preferred_element_type=jnp.float32)


def grads_kernel(*refs, scale, pairs, n_minor, n_major, carry):
    minor = refs[:n_minor]
    major = refs[n_minor:n_minor + n_major]
    noise_ref, spread_ref = refs[n_minor + n_major:n_minor + n_major + 2]
    rest = refs[n_minor + n_major + 2:]
    prev_ref = rest[0] if carry else None
    out_ref, acc_ref = rest[-2], rest[-1]
    step = pl.program_id(0)
    nb, width = acc_ref.shape[1], acc_ref.shape[2]

    @pl.when(step == 0)
    def _():
        acc_ref[...] = jnp.zeros_like(acc_ref)

    for b in range(nb):
        cols = slice(b * width, (b + 1) * width)
        for k, (f, lhs, rhs, flip) in enumerate(pairs):
            acc_ref[k, b] += nn_dot(minor[0][lhs, b], major[rhs][:, cols])

    @pl.when(step == pl.num_programs(0) - 1)
    def _():
        done = set()
        for k, (f, lhs, rhs, flip) in enumerate(pairs):
            done.add(f)
            for b in range(nb):
                grad = acc_ref[k, b]
                if flip:
                    grad = grad.T
                grad = grad * scale
                out_ref[0, f, b] = grad
                out_ref[1, f, b] = grad * noise_ref[f, b] * spread_ref[f, b]
        if carry:
            for f in range(noise_ref.shape[0]):
                if f not in done:
                    out_ref[:, f] = prev_ref[:, f]


def grads_and_curvature(minor, major, noise, spread, scale, pairs, prev=None):
    n_minor, nb, width, tokens = minor.shape
    feats = major[0].shape[1]
    tb = min(TOKEN_BLOCK, tokens)
    whole4 = pl.BlockSpec(noise.shape, lambda i: (0, 0, 0, 0))
    whole5 = pl.BlockSpec((2,) + noise.shape, lambda i: (0, 0, 0, 0, 0))
    in_specs = (
        [pl.BlockSpec((n_minor, nb, width, tb), lambda i: (0, 0, 0, i))]
        + [pl.BlockSpec((tb, feats), lambda i: (i, 0))] * len(major)
        + [whole4, whole4]
    )
    operands = [minor] + list(major) + [noise, spread]
    aliases = {}
    if prev is not None:
        in_specs.append(whole5)
        aliases = {len(operands): 0}
        operands.append(prev)
    kernel = functools.partial(
        grads_kernel, scale=scale, pairs=pairs, n_minor=1, n_major=len(major),
        carry=prev is not None,
    )
    return pl.pallas_call(
        kernel,
        grid=(tokens // tb,),
        in_specs=in_specs,
        out_specs=whole5,
        out_shape=jax.ShapeDtypeStruct((2,) + noise.shape, jnp.float32),
        scratch_shapes=[pltpu.VMEM((len(pairs), nb, width, width), jnp.float32)],
        input_output_aliases=aliases,
        compiler_params=pltpu.CompilerParams(dimension_semantics=("arbitrary",)),
    )(*operands)


def per_device(inputs, out_grad, mean_state, hess_state, grad_state, noise_draw):
    tokens = inputs.shape[0]
    local_blocks = mean_state.shape[1]
    width = mean_state.shape[3]
    groups = lax.axis_size("dp")
    scale = tokens ** (-0.5)
    full = gather_rows(jnp.stack([mean_state, hess_state]), groups)
    full_mean, full_hess = full[0], full[1]
    spread = jnp.sqrt(LAMBDA_SIZE * (full_hess + DELTA_DAMP))
    noise = noise_draw[0]
    sampled = (full_mean + noise / spread).astype(jnp.bfloat16)
    in_rows = inputs.reshape(tokens, local_blocks, width)
    grad_rows = out_grad.reshape(tokens, local_blocks, width)
    y_left = bdot("tbr,brc->tcb", in_rows, sampled[0]).astype(jnp.bfloat16)
    y_right = bdot("tbr,brc->tcb", in_rows, sampled[2]).astype(jnp.bfloat16)
    back_outer = bdot("tjc,jic->tij", grad_rows, sampled[5]).astype(jnp.bfloat16)
    first = lax.all_to_all(
        jnp.stack([y_left, y_right, back_outer], axis=1), "mp", split_axis=2, concat_axis=3, tiled=True
    )
    perm_left, perm_right, back_hidden = first[:, 0], first[:, 1], first[:, 2]
    u_left = bdot("tji,jic->tjc", perm_left, sampled[1])
    u_right = bdot("tji,jic->tjc", perm_right, sampled[3])
    hidden = (jax.nn.silu(u_left) * u_right).astype(jnp.bfloat16)
    outer = bdot("tbr,brc->tcb", hidden, sampled[4]).astype(jnp.bfloat16)
    d_hidden = bdot("tbc,brc->tbr", back_hidden, sampled[4])
    gate_grad = (d_hidden * u_right * silu_slope(u_left)).astype(jnp.bfloat16)
    value_grad = (d_hidden * jax.nn.silu(u_left)).astype(jnp.bfloat16)
    back_left = bdot("tjc,jic->tij", gate_grad, sampled[1]).astype(jnp.bfloat16)
    back_right = bdot("tjc,jic->tij", value_grad, sampled[3]).astype(jnp.bfloat16)
    token_minor = lambda a: jnp.moveaxis(a, 0, -1)
    flat = lambda a: a.reshape(tokens, -1)
    first_t = token_minor(first)
    early = grads_and_curvature(
        first_t, [flat(gate_grad), flat(value_grad), flat(hidden)],
        noise, spread, scale, pairs=((1, 0, 0, False), (3, 1, 1, False), (4, 2, 2, True)),
    )
    second = lax.all_to_all(
        jnp.stack([outer, back_left, back_right], axis=1), "mp", split_axis=2, concat_axis=3, tiled=True
    )
    second_t = token_minor(second)
    stacked = grads_and_curvature(
        second_t, [inputs, out_grad],
        noise, spread, scale, pairs=((0, 1, 0, True), (2, 2, 0, True), (5, 0, 1, False)), prev=early,
    )
    sums = scatter_rows(stacked, groups)
    grad_avg = sums[0] / groups
    hess_avg = sums[1] / groups
    new_grad = BETA_GRAD * grad_state + (1.0 - BETA_GRAD) * grad_avg
    new_hess = (
        BETA_HESS * hess_state
        + (1.0 - BETA_HESS) * hess_avg
        + 0.5 * (1.0 - BETA_HESS) ** 2 * (hess_state - hess_avg) ** 2 / (hess_state + DELTA_DAMP)
    )
    new_mean = mean_state - STEP_RATE * (new_grad + DELTA_DAMP * mean_state) / (
        new_hess + DELTA_DAMP
    )
    return (new_mean, new_hess, new_grad)


def solution(mesh):
    return jax.shard_map(
        per_device,
        mesh=mesh,
        in_specs=(
            P("dp", "mp"),
            P("dp", "mp"),
            P(None, "mp", "dp", None),
            P(None, "mp", "dp", None),
            P(None, "mp", "dp", None),
            P("dp", None, "mp", None, None),
        ),
        out_specs=(P(None, "mp", "dp", None), P(None, "mp", "dp", None), P(None, "mp", "dp", None)),
        check_vma=False,
    )
```

```python
import functools

import jax
import jax.numpy as jnp
from jax import lax
from jax.experimental import pallas as pl
from jax.experimental.pallas import tpu as pltpu
from jax.sharding import PartitionSpec as P

LAMBDA_SIZE = 100.0
DELTA_DAMP = 0.001
BETA_GRAD = 0.9
BETA_HESS = 0.9
STEP_RATE = 1.0

REDUCE_MODE = "a2a"


def bdot(form, left, right):
    return jnp.einsum(form, left, right, preferred_element_type=jnp.float32)


def silu_slope(value):
    sigm = jax.nn.sigmoid(value)
    return sigm * (1.0 + value * (1.0 - sigm))


def gather_rows(stacked, groups):
    shape = stacked.shape
    full = lax.all_gather(stacked.reshape(-1, 128), "dp", axis=0, tiled=True)
    full = jnp.moveaxis(full.reshape((groups,) + shape), 0, 3)
    return full.reshape(shape[:3] + (groups * shape[3], shape[4]))


def scatter_rows(stacked, groups):
    s, f, b, r, w = stacked.shape
    split = stacked.reshape(s, f, b, groups, r // groups, w)
    split = jnp.moveaxis(split, 3, 0)
    if REDUCE_MODE == "a2a":
        dense = split.reshape(groups, -1, 128)
        got = lax.all_to_all(dense, "dp", split_axis=0, concat_axis=0, tiled=True)
        summed = jnp.sum(got, axis=0).reshape(split.shape[1:])
    else:
        summed = lax.psum_scatter(split, "dp", scatter_dimension=0, tiled=False)
    return summed


TOKEN_BLOCK = 1024


def nn_dot(a, b):
    return lax.dot_general(a, b, (((1,), (0,)), ((), ())), preferred_element_type=jnp.float32)


def grads_kernel(*refs, scale, pairs, n_major, n_out, carry):
    minor_ref = refs[0]
    major = refs[1:1 + n_major]
    noise_refs = refs[1 + n_major:1 + n_major + n_out]
    spread_refs = refs[1 + n_major + n_out:1 + n_major + 2 * n_out]
    out_ref, acc_ref = refs[-2], refs[-1]
    step = pl.program_id(0)
    nb, width = acc_ref.shape[1], acc_ref.shape[2]

    @pl.when(step == 0)
    def _():
        acc_ref[...] = jnp.zeros_like(acc_ref)

    for b in range(nb):
        cols = slice(b * width, (b + 1) * width)
        for k, (q, lhs, rhs, flip) in enumerate(pairs):
            acc_ref[k, b] += nn_dot(minor_ref[lhs, b], major[rhs][:, cols])

    @pl.when(step == pl.num_programs(0) - 1)
    def _():
        for k, (q, lhs, rhs, flip) in enumerate(pairs):
            for b in range(nb):
                grad = acc_ref[k, b]
                if flip:
                    grad = grad.T
                grad = grad * scale
                out_ref[0, q, b] = grad
                out_ref[1, q, b] = grad * noise_refs[q][0, b] * spread_refs[q][0, b]


def grads_and_curvature(minor, major, noise, spread, scale, pairs, factors, half, prev=None):
    n_minor, nb, width, tokens = minor.shape
    feats = major[0].shape[1]
    tb = min(TOKEN_BLOCK, tokens)
    n_out = len(factors)
    picks = [pl.BlockSpec((1, nb, width, width), lambda i, f=f: (f, 0, 0, 0)) for f in factors]
    in_specs = (
        [pl.BlockSpec((n_minor, nb, width, tb), lambda i: (0, 0, 0, i))]
        + [pl.BlockSpec((tb, feats), lambda i: (i, 0))] * len(major)
        + picks + picks
    )
    operands = [minor] + list(major) + [noise] * n_out + [spread] * n_out
    aliases = {}
    if prev is not None:
        in_specs.append(pl.BlockSpec(memory_space=pl.ANY))
        aliases = {len(operands): 0}
        operands.append(prev)
    kernel = functools.partial(
        grads_kernel, scale=scale, pairs=pairs, n_major=len(major), n_out=n_out, carry=prev is not None,
    )
    return pl.pallas_call(
        kernel,
        grid=(tokens // tb,),
        in_specs=in_specs,
        out_specs=pl.BlockSpec((2, n_out, nb, width, width), lambda i: (0, half, 0, 0, 0)),
        out_shape=jax.ShapeDtypeStruct((2, 2 * n_out, nb, width, width), jnp.float32),
        scratch_shapes=[pltpu.VMEM((len(pairs), nb, width, width), jnp.float32)],
        input_output_aliases=aliases,
        compiler_params=pltpu.CompilerParams(dimension_semantics=("arbitrary",)),
    )(*operands)


def per_device(inputs, out_grad, mean_state, hess_state, grad_state, noise_draw):
    tokens = inputs.shape[0]
    local_blocks = mean_state.shape[1]
    width = mean_state.shape[3]
    groups = lax.axis_size("dp")
    scale = tokens ** (-0.5)
    full = gather_rows(jnp.stack([mean_state, hess_state]), groups)
    full_mean, full_hess = full[0], full[1]
    spread = jnp.sqrt(LAMBDA_SIZE * (full_hess + DELTA_DAMP))
    noise = noise_draw[0]
    sampled = (full_mean + noise / spread).astype(jnp.bfloat16)
    in_rows = inputs.reshape(tokens, local_blocks, width)
    grad_rows = out_grad.reshape(tokens, local_blocks, width)
    y_left = bdot("tbr,brc->tcb", in_rows, sampled[0]).astype(jnp.bfloat16)
    y_right = bdot("tbr,brc->tcb", in_rows, sampled[2]).astype(jnp.bfloat16)
    back_outer = bdot("tjc,jic->tij", grad_rows, sampled[5]).astype(jnp.bfloat16)
    first = lax.all_to_all(
        jnp.stack([y_left, y_right, back_outer], axis=1), "mp", split_axis=2, concat_axis=3, tiled=True
    )
    perm_left, perm_right, back_hidden = first[:, 0], first[:, 1], first[:, 2]
    u_left = bdot("tji,jic->tjc", perm_left, sampled[1])
    u_right = bdot("tji,jic->tjc", perm_right, sampled[3])
    hidden = (jax.nn.silu(u_left) * u_right).astype(jnp.bfloat16)
    outer = bdot("tbr,brc->tcb", hidden, sampled[4]).astype(jnp.bfloat16)
    d_hidden = bdot("tbc,brc->tbr", back_hidden, sampled[4])
    gate_grad = (d_hidden * u_right * silu_slope(u_left)).astype(jnp.bfloat16)
    value_grad = (d_hidden * jax.nn.silu(u_left)).astype(jnp.bfloat16)
    back_left = bdot("tjc,jic->tij", gate_grad, sampled[1]).astype(jnp.bfloat16)
    back_right = bdot("tjc,jic->tij", value_grad, sampled[3]).astype(jnp.bfloat16)
    token_minor = lambda a: jnp.moveaxis(a, 0, -1)
    flat = lambda a: a.reshape(tokens, -1)
    first_t = token_minor(first)
    early = grads_and_curvature(
        first_t, [flat(gate_grad), flat(value_grad), flat(hidden)],
        noise, spread, scale, pairs=((0, 0, 0, False), (1, 1, 1, False), (2, 2, 2, True)),
        factors=(1, 3, 4), half=1,
    )
    second = lax.all_to_all(
        jnp.stack([outer, back_left, back_right], axis=1), "mp", split_axis=2, concat_axis=3, tiled=True
    )
    second_t = token_minor(second)
    stacked = grads_and_curvature(
        second_t, [inputs, out_grad],
        noise, spread, scale, pairs=((0, 1, 0, True), (1, 2, 0, True), (2, 0, 1, False)),
        factors=(0, 2, 5), half=0, prev=early,
    )
    slots = scatter_rows(stacked, groups)
    sums = jnp.concatenate(
        [slots[:, 0:1], slots[:, 3:4], slots[:, 1:2], slots[:, 4:5], slots[:, 5:6], slots[:, 2:3]], axis=1
    )
    grad_avg = sums[0] / groups
    hess_avg = sums[1] / groups
    new_grad = BETA_GRAD * grad_state + (1.0 - BETA_GRAD) * grad_avg
    new_hess = (
        BETA_HESS * hess_state
        + (1.0 - BETA_HESS) * hess_avg
        + 0.5 * (1.0 - BETA_HESS) ** 2 * (hess_state - hess_avg) ** 2 / (hess_state + DELTA_DAMP)
    )
    new_mean = mean_state - STEP_RATE * (new_grad + DELTA_DAMP * mean_state) / (
        new_hess + DELTA_DAMP
    )
    return (new_mean, new_hess, new_grad)


def solution(mesh):
    return jax.shard_map(
        per_device,
        mesh=mesh,
        in_specs=(
            P("dp", "mp"),
            P("dp", "mp"),
            P(None, "mp", "dp", None),
            P(None, "mp", "dp", None),
            P(None, "mp", "dp", None),
            P("dp", None, "mp", None, None),
        ),
        out_specs=(P(None, "mp", "dp", None), P(None, "mp", "dp", None), P(None, "mp", "dp", None)),
        check_vma=False,
    )
```

```python
import functools

import jax
import jax.numpy as jnp
from jax import lax
from jax.experimental import pallas as pl
from jax.experimental.pallas import tpu as pltpu
from jax.sharding import PartitionSpec as P

LAMBDA_SIZE = 100.0
DELTA_DAMP = 0.001
BETA_GRAD = 0.9
BETA_HESS = 0.9
STEP_RATE = 1.0

REDUCE_MODE = "a2a"


def bdot(form, left, right):
    return jnp.einsum(form, left, right, preferred_element_type=jnp.float32)


def silu_slope(value):
    sigm = jax.nn.sigmoid(value)
    return sigm * (1.0 + value * (1.0 - sigm))


def gather_rows(stacked, groups):
    shape = stacked.shape
    full = lax.all_gather(stacked.reshape(-1, 128), "dp", axis=0, tiled=True)
    full = jnp.moveaxis(full.reshape((groups,) + shape), 0, 3)
    return full.reshape(shape[:3] + (groups * shape[3], shape[4]))


def scatter_rows(stacked, groups):
    s, f, b, r, w = stacked.shape
    split = stacked.reshape(s, f, b, groups, r // groups, w)
    split = jnp.moveaxis(split, 3, 0)
    if REDUCE_MODE == "a2a":
        dense = split.reshape(groups, -1, 128)
        got = lax.all_to_all(dense, "dp", split_axis=0, concat_axis=0, tiled=True)
        summed = jnp.sum(got, axis=0).reshape(split.shape[1:])
    else:
        summed = lax.psum_scatter(split, "dp", scatter_dimension=0, tiled=False)
    return summed


TOKEN_BLOCK = 1024


def nn_dot(a, b):
    return lax.dot_general(a, b, (((1,), (0,)), ((), ())), preferred_element_type=jnp.float32)


def grads_kernel(*refs, scale, pairs, n_major, n_out, carry):
    minor_ref = refs[0]
    major = refs[1:1 + n_major]
    noise_refs = refs[1 + n_major:1 + n_major + n_out]
    spread_refs = refs[1 + n_major + n_out:1 + n_major + 2 * n_out]
    out_ref, acc_ref = refs[-2], refs[-1]
    step = pl.program_id(0)
    nb, width = acc_ref.shape[1], acc_ref.shape[2]

    @pl.when(step == 0)
    def _():
        acc_ref[...] = jnp.zeros_like(acc_ref)

    for b in range(nb):
        cols = slice(b * width, (b + 1) * width)
        for k, (q, lhs, rhs, flip) in enumerate(pairs):
            acc_ref[k, b] += nn_dot(minor_ref[lhs, b], major[rhs][:, cols])

    @pl.when(step == pl.num_programs(0) - 1)
    def _():
        for k, (q, lhs, rhs, flip) in enumerate(pairs):
            for b in range(nb):
                grad = acc_ref[k, b]
                if flip:
                    grad = grad.T
                grad = grad * scale
                out_ref[0, q, b] = grad
                out_ref[1, q, b] = grad * noise_refs[q][0, b] * spread_refs[q][0, b]


def grads_and_curvature(minor, major, noise, spread, scale, pairs, factors, half, prev=None, block=TOKEN_BLOCK):
    n_minor, nb, width, tokens = minor.shape
    feats = major[0].shape[1]
    tb = min(block, tokens)
    n_out = len(factors)
    picks = [pl.BlockSpec((1, nb, width, width), lambda i, f=f: (f, 0, 0, 0)) for f in factors]
    in_specs = (
        [pl.BlockSpec((n_minor, nb, width, tb), lambda i: (0, 0, 0, i))]
        + [pl.BlockSpec((tb, feats), lambda i: (i, 0))] * len(major)
        + picks + picks
    )
    operands = [minor] + list(major) + [noise] * n_out + [spread] * n_out
    aliases = {}
    if prev is not None:
        in_specs.append(pl.BlockSpec(memory_space=pl.ANY))
        aliases = {len(operands): 0}
        operands.append(prev)
    kernel = functools.partial(
        grads_kernel, scale=scale, pairs=pairs, n_major=len(major), n_out=n_out, carry=prev is not None,
    )
    return pl.pallas_call(
        kernel,
        grid=(tokens // tb,),
        in_specs=in_specs,
        out_specs=pl.BlockSpec((2, n_out, nb, width, width), lambda i: (0, half, 0, 0, 0)),
        out_shape=jax.ShapeDtypeStruct((2, 2 * n_out, nb, width, width), jnp.float32),
        scratch_shapes=[pltpu.VMEM((len(pairs), nb, width, width), jnp.float32)],
        input_output_aliases=aliases,
        compiler_params=pltpu.CompilerParams(dimension_semantics=("arbitrary",)),
    )(*operands)


def per_device(inputs, out_grad, mean_state, hess_state, grad_state, noise_draw):
    tokens = inputs.shape[0]
    local_blocks = mean_state.shape[1]
    width = mean_state.shape[3]
    groups = lax.axis_size("dp")
    scale = tokens ** (-0.5)
    full = gather_rows(jnp.stack([mean_state, hess_state]), groups)
    full_mean, full_hess = full[0], full[1]
    spread = jnp.sqrt(LAMBDA_SIZE * (full_hess + DELTA_DAMP))
    noise = noise_draw[0]
    sampled = (full_mean + noise / spread).astype(jnp.bfloat16)
    in_rows = inputs.reshape(tokens, local_blocks, width)
    grad_rows = out_grad.reshape(tokens, local_blocks, width)
    y_left = bdot("tbr,brc->tcb", in_rows, sampled[0]).astype(jnp.bfloat16)
    y_right = bdot("tbr,brc->tcb", in_rows, sampled[2]).astype(jnp.bfloat16)
    back_outer = bdot("tjc,jic->tij", grad_rows, sampled[5]).astype(jnp.bfloat16)
    first = lax.all_to_all(
        jnp.stack([y_left, y_right, back_outer], axis=1), "mp", split_axis=2, concat_axis=3, tiled=True
    )
    perm_left, perm_right, back_hidden = first[:, 0], first[:, 1], first[:, 2]
    u_left = bdot("tji,jic->tjc", perm_left, sampled[1])
    u_right = bdot("tji,jic->tjc", perm_right, sampled[3])
    hidden = (jax.nn.silu(u_left) * u_right).astype(jnp.bfloat16)
    outer = bdot("tbr,brc->tcb", hidden, sampled[4]).astype(jnp.bfloat16)
    d_hidden = bdot("tbc,brc->tbr", back_hidden, sampled[4])
    gate_grad = (d_hidden * u_right * silu_slope(u_left)).astype(jnp.bfloat16)
    value_grad = (d_hidden * jax.nn.silu(u_left)).astype(jnp.bfloat16)
    back_left = bdot("tjc,jic->tij", gate_grad, sampled[1]).astype(jnp.bfloat16)
    back_right = bdot("tjc,jic->tij", value_grad, sampled[3]).astype(jnp.bfloat16)
    token_minor = lambda a: jnp.moveaxis(a, 0, -1)
    flat = lambda a: a.reshape(tokens, -1)
    first_t = token_minor(first)
    early = grads_and_curvature(
        first_t, [flat(gate_grad), flat(value_grad), flat(hidden)],
        noise, spread, scale, pairs=((0, 0, 0, False), (1, 1, 1, False), (2, 2, 2, True)),
        factors=(1, 3, 4), half=1,
    )
    second = lax.all_to_all(
        jnp.stack([outer, back_left, back_right], axis=1), "mp", split_axis=2, concat_axis=3, tiled=True
    )
    second_t = token_minor(second)
    stacked = grads_and_curvature(
        second_t, [inputs, out_grad],
        noise, spread, scale, pairs=((0, 1, 0, True), (1, 2, 0, True), (2, 0, 1, False)),
        factors=(0, 2, 5), half=0, prev=early, block=TOKEN_BLOCK // 2,
    )
    slots = scatter_rows(stacked, groups)
    sums = jnp.concatenate(
        [slots[:, 0:1], slots[:, 3:4], slots[:, 1:2], slots[:, 4:5], slots[:, 5:6], slots[:, 2:3]], axis=1
    )
    grad_avg = sums[0] / groups
    hess_avg = sums[1] / groups
    new_grad = BETA_GRAD * grad_state + (1.0 - BETA_GRAD) * grad_avg
    new_hess = (
        BETA_HESS * hess_state
        + (1.0 - BETA_HESS) * hess_avg
        + 0.5 * (1.0 - BETA_HESS) ** 2 * (hess_state - hess_avg) ** 2 / (hess_state + DELTA_DAMP)
    )
    new_mean = mean_state - STEP_RATE * (new_grad + DELTA_DAMP * mean_state) / (
        new_hess + DELTA_DAMP
    )
    return (new_mean, new_hess, new_grad)


def solution(mesh):
    return jax.shard_map(
        per_device,
        mesh=mesh,
        in_specs=(
            P("dp", "mp"),
            P("dp", "mp"),
            P(None, "mp", "dp", None),
            P(None, "mp", "dp", None),
            P(None, "mp", "dp", None),
            P("dp", None, "mp", None, None),
        ),
        out_specs=(P(None, "mp", "dp", None), P(None, "mp", "dp", None), P(None, "mp", "dp", None)),
        check_vma=False,
    )
```
